32 devices in a mesh: groups: 2 (over y), seq: 16 (over z, x, core).
Axes of the slice: x: 2, y: 2, z: 4, core: 2. Of those that a mesh axis runs over, the one named last changes fastest.
Arguments:
- queries: bfloat16 [4096, 3072], P(('groups', 'seq')), parts along dimension 0, may hold values from -8 to 8
- keys: bfloat16 [4096, 3072], P(('groups', 'seq')), parts along dimension 0, may hold values from -6 to 6
- values: bfloat16 [4096, 3072], P(('groups', 'seq')), parts along dimension 0, may hold values from -6 to 6
- rand_blocks: int32 [32, 3], P('groups'), parts along dimension 0, may hold values from 0 to 15, as said below
- global_ids: int32 [4], P('groups'), parts along dimension 0, may hold values from 0 to 15, as said below
Outputs:
- attended: bfloat16 [4096, 3072], P(('groups', 'seq')), parts along dimension 0
The draws below stay inside these ranges and needn't reach their ends.
There are 2 independent parts, one for each index of `groups`. The reference program is written for one: setup_inputs(seed, part) draws one part's arguments, and reference() takes and returns one part's arrays. A program takes and returns all parts, laid end to end along the dimension named above; each array names one. Nothing has to cross between parts.
Inputs may be any that keep to these rules, and one draw needn't show every extreme that they name: `rand_blocks`: row b names 3 different blocks, none of them b-1, b, b+1 or a global block. `global_ids`: 2 different blocks, one of which is the last block.
All inputs are finite; a program needn't handle non-finite values.
Results may differ from the reference program's by a relative error of at most 0.0049.
Values may be sent and summed in bfloat16 or wider, within the bound.
A program may use at most 128 MiB of HBM per device.

```python
import jax
import jax.numpy as jnp
from jax import lax

HEADS = 24
HEAD_DIM = 128
BLOCK = 128
GLOBALS = 2
RANDOMS = 3
WIDTH = 3072
NBLOCKS = 16
TOKENS = 2048


def query_key_pair(key):
    base_queries = jax.random.normal(jax.random.fold_in(key, 101), (TOKENS, WIDTH), jnp.float32)
    base_keys = jax.random.normal(jax.random.fold_in(key, 102), (TOKENS, WIDTH), jnp.float32)
    drawn_queries = 2.2 * jnp.clip(base_queries, -2.7, 2.7)
    drawn_keys = jnp.clip(base_keys, -4.0, 4.0)
    return (drawn_queries, drawn_keys)


def draw_queries(key, part):
    return query_key_pair(key)[0].astype(jnp.bfloat16)


def draw_keys(key, part):
    return query_key_pair(key)[1].astype(jnp.bfloat16)


def block_tables(key):
    others = jax.random.permutation(jax.random.fold_in(key, 201), NBLOCKS - 1)[:GLOBALS - 1].astype(jnp.int32)
    chosen_globals = jnp.concatenate([others, jnp.full((1,), NBLOCKS - 1, dtype=jnp.int32)]).astype(jnp.int32)
    columns = jnp.arange(NBLOCKS, dtype=jnp.int32)
    rows = columns[:, None]
    scores = jax.random.randint(jax.random.fold_in(key, 202), (NBLOCKS, NBLOCKS), 0, 2 ** 20, dtype=jnp.int32) * NBLOCKS + columns[None, :]
    near = jnp.abs(columns[None, :] - rows) <= 1
    global_column = jnp.any(columns[:, None] == chosen_globals[None, :], axis=1)[None, :]
    scores = jnp.where(near | global_column, -1, scores)
    picked = lax.top_k(scores, RANDOMS)[1].astype(jnp.int32)
    return (picked, chosen_globals)


def draw_rand_blocks(key, part):
    return block_tables(key)[0]


def draw_global_ids(key, part):
    return block_tables(key)[1]


def level_of(own_key, extent, split, low, largest):
    loudness, own = 1.0, jax.random.fold_in(own_key, 6)
    for axis_at, parts in split:
        draws = jnp.exp(jax.random.uniform(jax.random.fold_in(own, axis_at), (parts,), jnp.float32, low / len(split), largest / len(split)))
        loudness = loudness * jnp.repeat(draws, extent[axis_at] // parts).reshape([-1 if axis == axis_at else 1 for axis in range(len(extent))])
    return loudness


def normal_values(stream_key, shape, width, bound, split=(), kind=jnp.bfloat16):
    values = jax.random.normal(stream_key, shape, jnp.float32) * width
    if len(split) > 0:
        values = level_of(stream_key, shape, split, -0.22, 0.18) * values
    return jnp.clip(values, min=-bound, max=bound).astype(kind)


def setup_inputs(seed: int = 0, part: int = 0) -> dict:
    key_of = jax.random.split(jax.random.key(seed), 6)
    own_keys = jax.random.split(jax.random.fold_in(key_of[5], part), 6)
    return {
        "queries": draw_queries(jax.random.fold_in(jax.random.fold_in(key_of[5], part), 71), part),
        "keys": draw_keys(jax.random.fold_in(jax.random.fold_in(key_of[5], part), 71), part),
        "values": normal_values(own_keys[2], (TOKENS, WIDTH), 1.0, 6.0, ((0, 16),)),
        "rand_blocks": draw_rand_blocks(jax.random.fold_in(jax.random.fold_in(key_of[5], part), 71), part),
        "global_ids": draw_global_ids(jax.random.fold_in(jax.random.fold_in(key_of[5], part), 71), part),
    }


def reference(queries, keys, values, rand_blocks, global_ids):
    query_blocks = queries.reshape(NBLOCKS, BLOCK, HEADS, HEAD_DIM)
    key_blocks = keys.reshape(NBLOCKS, BLOCK, HEADS, HEAD_DIM)
    value_blocks = values.reshape(NBLOCKS, BLOCK, HEADS, HEAD_DIM)
    scale = HEAD_DIM ** -0.5

    def one_block(block_id):
        window = block_id + jnp.arange(-1, 2, dtype=jnp.int32)
        global_hit = jnp.any(window[:, None] == global_ids[None, :], axis=1)
        window_ok = (window >= 0) & (window < NBLOCKS) & jnp.logical_not(global_hit)
        wanted = jnp.concatenate([window, global_ids.astype(jnp.int32), rand_blocks[block_id].astype(jnp.int32)])
        usable = jnp.concatenate([window_ok, jnp.ones((GLOBALS + RANDOMS,), dtype=bool)])
        index = jnp.clip(wanted, 0, NBLOCKS - 1).astype(jnp.int32)
        chosen_keys = key_blocks[index].astype(jnp.float32)
        chosen_values = value_blocks[index].astype(jnp.float32)
        own_queries = query_blocks[block_id].astype(jnp.float32)
        scores = jnp.einsum('qhd,jkhd->hqjk', own_queries, chosen_keys) * scale
        scores = jnp.where(usable[None, None, :, None], scores, -1e30)
        top = jnp.max(scores, axis=(2, 3), keepdims=True)
        powers = jnp.exp(scores - top)
        total = jnp.sum(powers, axis=(2, 3), keepdims=True)
        probs = (powers / total).astype(jnp.bfloat16)
        result = jnp.einsum('hqjk,jkhd->qhd', probs.astype(jnp.float32), chosen_values)
        return result.reshape(BLOCK, WIDTH).astype(jnp.bfloat16)

    outputs = lax.map(one_block, jnp.arange(NBLOCKS, dtype=jnp.int32))
    return outputs.reshape(TOKENS, WIDTH)
```

```python
import functools

import jax
import jax.numpy as jnp
from jax import lax
from jax.experimental import pallas as pl
from jax.experimental.pallas import tpu as pltpu
from jax.sharding import PartitionSpec as P

HEADS = 24
HEAD_DIM = 128
BLOCK = 128
GLOBALS = 2
RANDOMS = 3
LOCAL_HEADS = 3
GROUPS = HEADS // LOCAL_HEADS
MESH = pl.DeviceIdType.MESH
NEG = -1e30


def kernel(ranks, rand_ref, glob_ref, q_hbm, k_hbm, v_hbm, out_hbm, qs, os, *scratch):
    kvs = scratch[:LOCAL_HEADS]
    (send_sem, q_recv, kv_recv, fwd_send, fwd_recv, out_send, out_recv, late_sem) = scratch[LOCAL_HEADS:]
    rollout = lax.axis_index("groups")
    me = lax.axis_index("seq")
    group, rank = lax.div(me, ranks), lax.rem(me, ranks)
    blocks = ranks * GROUPS

    def for_peers(body):
        @pl.loop(0, GROUPS - 1)
        def _(j):
            body(j + jnp.where(j >= group, 1, 0))

    def sibling(i):
        return group * ranks + lax.rem(rank + i, ranks)

    def device(index):
        return (rollout, index)

    barrier = pltpu.get_barrier_semaphore()

    late_from = GROUPS - GROUPS // 4
    late = group >= late_from

    @for_peers
    def _(p):
        @pl.when(jnp.logical_not(late) | (p >= late_from))
        def _():
            pl.semaphore_signal(barrier, inc=1, device_id=device(p * ranks + rank), device_id_type=MESH)

    @pl.loop(1, ranks)
    def _(i):
        pl.semaphore_signal(barrier, inc=1, device_id=device(sibling(i)), device_id_type=MESH)

    pl.semaphore_wait(barrier, jnp.where(late, GROUPS, late_from) - 1 + ranks - 1)

    @pl.when(late)
    def _():
        @pl.loop(0, late_from)
        def _(p):
            pl.semaphore_signal(late_sem, inc=1, device_id=device(p * ranks + rank), device_id_type=MESH)

    sources = (q_hbm, k_hbm, v_hbm)

    def columns(owner, h):
        start = pl.multiple_of((owner * LOCAL_HEADS + h) * HEAD_DIM, HEAD_DIM)
        return pl.ds(start, HEAD_DIM)

    def slab(t, h, owner_group):
        if t == 0:
            return qs.at[h, owner_group]
        return kvs[h].at[owner_group * ranks + rank, t - 1]

    def arrival(t, h, owner_group):
        return q_recv.at[h] if t == 0 else kv_recv.at[h, owner_group]

    def send(t, h, p):
        return pltpu.make_async_remote_copy(
            src_ref=sources[t].at[:, columns(p, h)],
            dst_ref=slab(t, h, group),
            send_sem=send_sem.at[t],
            recv_sem=arrival(t, h, group),
            device_id=device(p * ranks + rank),
            device_id_type=MESH,
        )

    def own(t, h):
        return pltpu.make_async_copy(
            sources[t].at[:, columns(group, h)], slab(t, h, group), arrival(t, h, group)
        )

    def forward(h, p, i):
        here = kvs[h].at[p * ranks + rank]
        return pltpu.make_async_remote_copy(
            src_ref=here,
            dst_ref=here,
            send_sem=fwd_send.at[h, i - 1],
            recv_sem=fwd_recv.at[h],
            device_id=device(sibling(i)),
            device_id_type=MESH,
        )

    def send_out(h, p):
        return pltpu.make_async_remote_copy(
            src_ref=os.at[h, p],
            dst_ref=out_hbm.at[:, columns(group, h)],
            send_sem=out_send,
            recv_sem=out_recv,
            device_id=device(p * ranks + rank),
            device_id_type=MESH,
        )

    def out_local(h):
        return pltpu.make_async_copy(os.at[h, group], out_hbm.at[:, columns(group, h)], out_recv)

    def wait_bytes(ref, sem):
        pltpu.make_async_copy(ref, ref, sem).wait()

    for h in range(LOCAL_HEADS):
        @for_peers
        def _(p):
            @pl.when(late | (p < late_from) | (h > 0))
            def _():
                for t in (1, 2, 0):
                    send(t, h, p).start()

        if h == 0:
            @pl.when(jnp.logical_not(late))
            def _():
                pl.semaphore_wait(late_sem, GROUPS - late_from)

                @pl.loop(late_from, GROUPS)
                def _(p):
                    for t in (1, 2, 0):
                        send(t, h, p).start()

        for t in (1, 2, 0):
            own(t, h).start()

    def attend(h, slot):
        block = slot * ranks + rank
        g0, g1 = glob_ref[0], glob_ref[1]

        def bias(b, inside):
            ok = inside & (b != g0) & (b != g1)
            return jnp.where(ok, jnp.float32(0.0), jnp.float32(NEG))

        ids = [
            jnp.maximum(block - 1, 0),
            block,
            jnp.minimum(block + 1, blocks - 1),
            g0,
            g1,
        ] + [rand_ref[r, block] for r in range(RANDOMS)]
        biases = [
            bias(block - 1, block >= 1),
            bias(block, block >= 0),
            bias(block + 1, block + 1 < blocks),
        ]
        query = qs[h, slot]
        key = jnp.concatenate([kvs[h][i, 0] for i in ids], axis=0)
        value = jnp.concatenate([kvs[h][i, 1] for i in ids], axis=0)
        scores = lax.dot_general(
            query, key, (((1,), (1,)), ((), ())), preferred_element_type=jnp.float32
        ) * (HEAD_DIM ** -0.5)
        parts = [scores[:, n * BLOCK : (n + 1) * BLOCK] for n in range(len(ids))]
        parts = [part + biases[n] if n < 3 else part for n, part in enumerate(parts)]
        top = jnp.max(functools.reduce(jnp.maximum, parts), axis=1, keepdims=True)
        powers = [jnp.exp(part - top) for part in parts]
        total = jnp.sum(functools.reduce(jnp.add, powers), axis=1, keepdims=True)
        inverse = 1.0 / total
        probs = jnp.concatenate([(power * inverse).astype(jnp.bfloat16) for power in powers], axis=1)
        result = lax.dot_general(
            probs, value, (((1,), (0,)), ((), ())), preferred_element_type=jnp.float32
        )
        os[h, slot] = result.astype(jnp.bfloat16)

    for h in range(LOCAL_HEADS):
        def pass_on(p):
            wait_bytes(kvs[h].at[p * ranks + rank], kv_recv.at[h, p])

            @pl.loop(1, ranks)
            def _(i):
                forward(h, p, i).start()

        pass_on(group)
        for_peers(pass_on)
        wait_bytes(qs.at[h], q_recv.at[h])
        wait_bytes(kvs[h].at[pl.ds(0, (ranks - 1) * GROUPS)], fwd_recv.at[h])

        @pl.loop(0, GROUPS)
        def _(p):
            attend(h, p)

            @pl.when(p != group)
            def _():
                send_out(h, p).start()

        out_local(h).start()

    sent = os.at[:, pl.ds(0, GROUPS - 1)]
    for t in (1, 2, 0):
        wait_bytes(sent, send_sem.at[t])

    @pl.loop(1, ranks)
    def _(i):
        for h in range(LOCAL_HEADS):
            wait_bytes(kvs[h].at[pl.ds(0, GROUPS)], fwd_send.at[h, i - 1])

    wait_bytes(sent, out_send)
    wait_bytes(out_hbm, out_recv)


def local(queries, keys, values, rand_blocks, global_ids):
    seq = lax.axis_size("seq")
    ranks = seq // GROUPS
    blocks = rand_blocks.shape[0]
    assert queries.shape[0] == BLOCK and blocks == seq and seq % GROUPS == 0
    tile = (BLOCK, HEAD_DIM)
    sources = [pltpu.with_memory_space_constraint(x, pltpu.MemorySpace.HBM) for x in (rand_blocks.T, global_ids, queries, keys, values)]
    anywhere = pl.BlockSpec(memory_space=pl.ANY)
    scalars = pl.BlockSpec(memory_space=pltpu.SMEM)
    dma = pltpu.SemaphoreType.DMA
    return pl.pallas_call(
        functools.partial(kernel, ranks),
        out_shape=jax.ShapeDtypeStruct(queries.shape, jnp.bfloat16),
        in_specs=[scalars, scalars, anywhere, anywhere, anywhere],
        out_specs=anywhere,
        scratch_shapes=[
            pltpu.VMEM((LOCAL_HEADS, GROUPS) + tile, jnp.bfloat16),
            pltpu.VMEM((LOCAL_HEADS, GROUPS) + tile, jnp.bfloat16),
        ]
        + [pltpu.VMEM((blocks, 2) + tile, jnp.bfloat16)] * LOCAL_HEADS
        + [
            dma((3,)),
            dma((LOCAL_HEADS,)),
            dma((LOCAL_HEADS, GROUPS)),
            dma((LOCAL_HEADS, ranks - 1)),
            dma((LOCAL_HEADS,)),
            dma,
            dma,
            pltpu.SemaphoreType.REGULAR,
        ],
        compiler_params=pltpu.CompilerParams(
            collective_id=0, has_side_effects=True, vmem_limit_bytes=40 << 20
        ),
    )(*sources)


def solution(mesh):
    placed = (
        P(("groups", "seq"), None),
        P(("groups", "seq"), None),
        P(("groups", "seq"), None),
        P("groups", None),
        P("groups"),
    )
    return jax.shard_map(
        local, mesh=mesh, in_specs=placed, out_specs=P(("groups", "seq"), None), check_vma=False
    )
```

```python
import functools

import jax
import jax.numpy as jnp
from jax import lax
from jax.experimental import pallas as pl
from jax.experimental.pallas import tpu as pltpu
from jax.sharding import PartitionSpec as P

HEADS = 24
HEAD_DIM = 128
BLOCK = 128
GLOBALS = 2
RANDOMS = 3
LOCAL_HEADS = 3
GROUPS = HEADS // LOCAL_HEADS
MESH = pl.DeviceIdType.MESH
NEG = -1e30


def swapped(p):
    return p + jnp.where(p == GROUPS // 2 - 1, 1, 0) - jnp.where(p == GROUPS // 2, 1, 0)


def kernel(ranks, rand_hbm, glob_hbm, q_hbm, k_hbm, v_hbm, out_hbm, qs, os, rand_ref, glob_ref, *scratch):
    kvs = scratch[:LOCAL_HEADS]
    (table_sem, send_sem, q_recv, kv_recv, fwd_send, fwd_recv, out_send, out_recv, ready) = scratch[LOCAL_HEADS:]
    rollout = lax.axis_index("groups")
    me = lax.axis_index("seq")
    group, rank = lax.div(me, ranks), lax.rem(me, ranks)
    blocks = ranks * GROUPS
    place = swapped(group)
    pair = lax.div(place, 2)

    def sibling(i):
        return group * ranks + lax.rem(rank + i, ranks)

    def device(index):
        return (rollout, index)

    barrier = pltpu.get_barrier_semaphore()

    @pl.loop(1, ranks)
    def _(i):
        pl.semaphore_signal(barrier, inc=1, device_id=device(sibling(i)), device_id_type=MESH)

    @pl.loop(2 * pair, GROUPS)
    def _(at):
        @pl.when(at != place)
        def _():
            pl.semaphore_signal(barrier, inc=1, device_id=device(swapped(at) * ranks + rank), device_id_type=MESH)

    tables = (
        pltpu.make_async_copy(rand_hbm, rand_ref, table_sem.at[0]),
        pltpu.make_async_copy(glob_hbm, glob_ref, table_sem.at[1]),
    )
    for table in tables:
        table.start()

    sources = (q_hbm, k_hbm, v_hbm)

    def columns(owner, h):
        start = pl.multiple_of((owner * LOCAL_HEADS + h) * HEAD_DIM, HEAD_DIM)
        return pl.ds(start, HEAD_DIM)

    def slab(t, h, owner_group):
        if t == 0:
            return qs.at[h, owner_group]
        return kvs[h].at[rank * GROUPS + owner_group, t - 1]

    def arrival(t, h):
        return (q_recv if t == 0 else kv_recv).at[h]

    def send(h, p):
        for t in (1, 2, 0):
            pltpu.make_async_remote_copy(
                src_ref=sources[t].at[:, columns(p, h)],
                dst_ref=slab(t, h, group),
                send_sem=send_sem.at[t],
                recv_sem=arrival(t, h),
                device_id=device(p * ranks + rank),
                device_id_type=MESH,
            ).start()

    def own(h):
        for t in (1, 2, 0):
            pltpu.make_async_copy(
                sources[t].at[:, columns(group, h)], slab(t, h, group), arrival(t, h)
            ).start()

    def mine(h):
        return kvs[h].at[pl.ds(rank * GROUPS, GROUPS)]

    def forward(h, i):
        pltpu.make_async_remote_copy(
            src_ref=mine(h),
            dst_ref=mine(h),
            send_sem=fwd_send.at[h, i - 1],
            recv_sem=fwd_recv.at[h],
            device_id=device(sibling(i)),
            device_id_type=MESH,
        ).start()

    def send_out(h, p):
        pltpu.make_async_remote_copy(
            src_ref=os.at[h, p],
            dst_ref=out_hbm.at[:, columns(group, h)],
            send_sem=out_send,
            recv_sem=out_recv,
            device_id=device(p * ranks + rank),
            device_id_type=MESH,
        ).start()

    def out_local(h):
        pltpu.make_async_copy(os.at[h, group], out_hbm.at[:, columns(group, h)], out_recv).start()

    def wait_bytes(ref, sem):
        pltpu.make_async_copy(ref, ref, sem).wait()

    def far_first(body):
        @pl.loop(0, GROUPS)
        def _(j):
            p = lax.rem(j + jnp.where(group < GROUPS // 2, GROUPS // 2, 0), GROUPS)
            body(p)

    pl.semaphore_wait(barrier, 2 * pair + 1 + ranks - 1)

    @pl.loop(0, 2 * pair)
    def _(at):
        pl.semaphore_signal(ready.at[pair], inc=1, device_id=device(swapped(at) * ranks + rank), device_id_type=MESH)

    @pl.loop(0, 2 * pair + 2)
    def _(j):
        at = 2 * pair + 1 - j

        @pl.when(at != place)
        def _():
            send(0, swapped(at))

    own(0)

    @pl.loop(pair + 1, GROUPS // 2)
    def _(later):
        pl.semaphore_wait(ready.at[later], 2)

        @pl.loop(2 * later, 2 * later + 2)
        def _(at):
            send(0, swapped(at))

    for h in range(1, LOCAL_HEADS):
        def send_others(p):
            @pl.when(p != group)
            def _():
                send(h, p)

        far_first(send_others)
        own(h)

    for table in tables:
        table.wait()

    def attend(h, slot):
        block = slot * ranks + rank
        g0, g1 = glob_ref[0], glob_ref[1]

        def bias(b, inside):
            ok = inside & (b != g0) & (b != g1)
            return jnp.where(ok, jnp.float32(0.0), jnp.float32(NEG))

        ids = [
            jnp.maximum(block - 1, 0),
            block,
            jnp.minimum(block + 1, blocks - 1),
            g0,
            g1,
        ] + [rand_ref[r, block] for r in range(RANDOMS)]
        biases = [
            bias(block - 1, block >= 1),
            bias(block, block >= 0),
            bias(block + 1, block + 1 < blocks),
        ]
        query = qs[h, slot]
        slots = [lax.rem(i, ranks) * GROUPS + lax.div(i, ranks) for i in ids]
        key = jnp.concatenate([kvs[h][i, 0] for i in slots], axis=0)
        value = jnp.concatenate([kvs[h][i, 1] for i in slots], axis=0)
        scores = lax.dot_general(
            query, key, (((1,), (1,)), ((), ())), preferred_element_type=jnp.float32
        ) * (HEAD_DIM ** -0.5)
        parts = [scores[:, n * BLOCK : (n + 1) * BLOCK] for n in range(len(ids))]
        parts = [part + biases[n] if n < 3 else part for n, part in enumerate(parts)]
        top = jnp.max(functools.reduce(jnp.maximum, parts), axis=1, keepdims=True)
        powers = [jnp.exp(part - top) for part in parts]
        total = jnp.sum(functools.reduce(jnp.add, powers), axis=1, keepdims=True)
        inverse = 1.0 / total
        probs = jnp.concatenate([(power * inverse).astype(jnp.bfloat16) for power in powers], axis=1)
        result = lax.dot_general(
            probs, value, (((1,), (0,)), ((), ())), preferred_element_type=jnp.float32
        )
        os[h, slot] = result.astype(jnp.bfloat16)

    for h in range(LOCAL_HEADS):
        wait_bytes(mine(h), kv_recv.at[h])

        @pl.loop(1, ranks)
        def _(i):
            forward(h, i)

        wait_bytes(qs.at[h], q_recv.at[h])
        wait_bytes(kvs[h].at[pl.ds(0, (ranks - 1) * GROUPS)], fwd_recv.at[h])

        def attend_and_send(p):
            attend(h, p)

            @pl.when(p != group)
            def _():
                send_out(h, p)

        far_first(attend_and_send)
        out_local(h)

    sent = os.at[:, pl.ds(0, GROUPS - 1)]
    for t in (1, 2, 0):
        wait_bytes(sent, send_sem.at[t])

    @pl.loop(1, ranks)
    def _(i):
        for h in range(LOCAL_HEADS):
            wait_bytes(mine(h), fwd_send.at[h, i - 1])

    wait_bytes(sent, out_send)
    wait_bytes(out_hbm, out_recv)


def local(queries, keys, values, rand_blocks, global_ids):
    seq = lax.axis_size("seq")
    ranks = seq // GROUPS
    blocks = rand_blocks.shape[0]
    assert queries.shape[0] == BLOCK and blocks == seq and seq % GROUPS == 0
    tile = (BLOCK, HEAD_DIM)
    sources = [pltpu.with_memory_space_constraint(x, pltpu.MemorySpace.HBM) for x in (rand_blocks.T, global_ids, queries, keys, values)]
    anywhere = pl.BlockSpec(memory_space=pl.ANY)
    dma = pltpu.SemaphoreType.DMA
    return pl.pallas_call(
        functools.partial(kernel, ranks),
        out_shape=jax.ShapeDtypeStruct(queries.shape, jnp.bfloat16),
        in_specs=[anywhere] * 5,
        out_specs=anywhere,
        scratch_shapes=[
            pltpu.VMEM((LOCAL_HEADS, GROUPS) + tile, jnp.bfloat16),
            pltpu.VMEM((LOCAL_HEADS, GROUPS) + tile, jnp.bfloat16),
            pltpu.SMEM((RANDOMS, blocks), jnp.int32),
            pltpu.SMEM((GLOBALS,), jnp.int32),
        ]
        + [pltpu.VMEM((blocks, 2) + tile, jnp.bfloat16)] * LOCAL_HEADS
        + [
            dma((2,)),
            dma((3,)),
            dma((LOCAL_HEADS,)),
            dma((LOCAL_HEADS,)),
            dma((LOCAL_HEADS, ranks - 1)),
            dma((LOCAL_HEADS,)),
            dma,
            dma,
            pltpu.SemaphoreType.REGULAR((GROUPS // 2,)),
        ],
        compiler_params=pltpu.CompilerParams(
            collective_id=0, has_side_effects=True, vmem_limit_bytes=40 << 20
        ),
    )(*sources)


def solution(mesh):
    placed = (
        P(("groups", "seq"), None),
        P(("groups", "seq"), None),
        P(("groups", "seq"), None),
        P("groups", None),
        P("groups"),
    )
    return jax.shard_map(
        local, mesh=mesh, in_specs=placed, out_specs=P(("groups", "seq"), None), check_vma=False
    )
```

```python
import functools

import jax
import jax.numpy as jnp
from jax import lax
from jax.experimental import pallas as pl
from jax.experimental.pallas import tpu as pltpu
from jax.sharding import PartitionSpec as P

HEADS = 24
HEAD_DIM = 128
BLOCK = 128
GLOBALS = 2
RANDOMS = 3
LOCAL_HEADS = 3
GROUPS = HEADS // LOCAL_HEADS
MESH = pl.DeviceIdType.MESH
NEG = -1e30


SENDS = (
    (6, 7, 4, 5, 2, 3, 1, 0),
    (7, 6, 4, 5, 3, 2, 0, 1),
    (6, 7, 4, 5, 0, 1, 3, 2),
    (6, 7, 4, 5, 0, 1, 2, 3),
    (0, 1, 2, 3, 6, 7, 5, 4),
    (0, 1, 2, 3, 6, 7, 4, 5),
    (0, 1, 2, 3, 4, 5, 7, 6),
    (0, 1, 2, 3, 4, 5, 6, 7),
)
RESULTS = (
    (4, 6, 5, 7, 2, 1, 3, 0),
    (4, 6, 5, 7, 0, 2, 3, 1),
    (0, 1, 4, 6, 7, 5, 3, 2),
    (0, 2, 1, 4, 6, 5, 7, 3),
    (0, 1, 2, 3, 6, 7, 5, 4),
    (0, 1, 2, 3, 6, 7, 4, 5),
    (0, 1, 2, 3, 4, 5, 7, 6),
    (0, 1, 2, 3, 4, 5, 6, 7),
)
HELD = (2, 3)


def swapped(p):
    return p + jnp.where(p == GROUPS // 2 - 1, 1, 0) - jnp.where(p == GROUPS // 2, 1, 0)


def kernel(ranks, rand_hbm, glob_hbm, q_hbm, k_hbm, v_hbm, out_hbm, qs, os, rand_ref, glob_ref, *scratch):
    kvs = scratch[:LOCAL_HEADS]
    (table_sem, send_sem, q_recv, kv_recv, fwd_send, fwd_recv, out_send, out_recv, ready) = scratch[LOCAL_HEADS:]
    rollout = lax.axis_index("groups")
    me = lax.axis_index("seq")
    group, rank = lax.div(me, ranks), lax.rem(me, ranks)
    blocks = ranks * GROUPS
    place = swapped(group)
    pair = lax.div(place, 2)

    def sibling(i):
        return group * ranks + lax.rem(rank + i, ranks)

    def device(index):
        return (rollout, index)

    barrier = pltpu.get_barrier_semaphore()

    @pl.loop(1, ranks)
    def _(i):
        pl.semaphore_signal(barrier, inc=1, device_id=device(sibling(i)), device_id_type=MESH)

    @pl.loop(2 * pair, GROUPS)
    def _(at):
        @pl.when(at != place)
        def _():
            pl.semaphore_signal(barrier, inc=1, device_id=device(swapped(at) * ranks + rank), device_id_type=MESH)

    tables = (
        pltpu.make_async_copy(rand_hbm, rand_ref, table_sem.at[0]),
        pltpu.make_async_copy(glob_hbm, glob_ref, table_sem.at[1]),
    )
    for table in tables:
        table.start()

    sources = (q_hbm, k_hbm, v_hbm)

    def columns(owner, h):
        start = pl.multiple_of((owner * LOCAL_HEADS + h) * HEAD_DIM, HEAD_DIM)
        return pl.ds(start, HEAD_DIM)

    def slab(t, h, owner_group):
        if t == 0:
            return qs.at[h, owner_group]
        return kvs[h].at[rank * GROUPS + owner_group, t - 1]

    def send(h, p, which=(1, 2, 0)):
        for t in which:
            pltpu.make_async_remote_copy(
                src_ref=sources[t].at[:, columns(p, h)],
                dst_ref=slab(t, h, group),
                send_sem=send_sem.at[t],
                recv_sem=(q_recv if t == 0 else kv_recv).at[h],
                device_id=device(p * ranks + rank),
                device_id_type=MESH,
            ).start()

    def own(h):
        for t in (1, 2, 0):
            pltpu.make_async_copy(
                sources[t].at[:, columns(group, h)], slab(t, h, group), (q_recv if t == 0 else kv_recv).at[h]
            ).start()

    def mine(h):
        return kvs[h].at[pl.ds(rank * GROUPS, GROUPS)]

    def forward(h, i):
        pltpu.make_async_remote_copy(
            src_ref=mine(h),
            dst_ref=mine(h),
            send_sem=fwd_send.at[h, i - 1],
            recv_sem=fwd_recv.at[h],
            device_id=device(sibling(i)),
            device_id_type=MESH,
        ).start()

    def send_out(h, p):
        pltpu.make_async_remote_copy(
            src_ref=os.at[h, p],
            dst_ref=out_hbm.at[:, columns(group, h)],
            send_sem=out_send,
            recv_sem=out_recv,
            device_id=device(p * ranks + rank),
            device_id_type=MESH,
        ).start()

    def out_local(h):
        pltpu.make_async_copy(os.at[h, group], out_hbm.at[:, columns(group, h)], out_recv).start()

    def wait_bytes(ref, sem):
        pltpu.make_async_copy(ref, ref, sem).wait()

    def in_order(rows, body):
        codes = [sum(p << 3 * k for k, p in enumerate(row)) for row in rows]
        code = functools.reduce(lambda rest, g: jnp.where(group == g, codes[g], rest), range(1, GROUPS), codes[0])

        @pl.loop(0, GROUPS)
        def _(k):
            body(lax.shift_right_logical(code, 3 * k) & 7)

    pl.semaphore_wait(barrier, 2 * pair + 1 + ranks - 1)

    @pl.loop(0, 2 * pair)
    def _(at):
        pl.semaphore_signal(ready.at[pair], inc=1, device_id=device(swapped(at) * ranks + rank), device_id_type=MESH)

    @pl.loop(0, 2 * pair + 2)
    def _(j):
        at = 2 * pair + 1 - j

        @pl.when(at != place)
        def _():
            send(0, swapped(at))

    own(0)

    @pl.loop(pair + 1, GROUPS // 2)
    def _(later):
        pl.semaphore_wait(ready.at[later], 2)

        @pl.loop(2 * later, 2 * later + 2)
        def _(at):
            send(0, swapped(at))

    for h, which in ((1, (1, 2, 0)), (2, (1, 2)), (2, (0,))):
        def send_others(p):
            @pl.when(p != group)
            def _():
                send(h, p, which)

        in_order(SENDS, send_others)
        if 0 in which:
            own(h)

    for table in tables:
        table.wait()

    def attend(h, slot):
        block = slot * ranks + rank
        g0, g1 = glob_ref[0], glob_ref[1]

        def bias(b, inside):
            ok = inside & (b != g0) & (b != g1)
            return jnp.where(ok, jnp.float32(0.0), jnp.float32(NEG))

        ids = [
            jnp.maximum(block - 1, 0),
            block,
            jnp.minimum(block + 1, blocks - 1),
            g0,
            g1,
        ] + [rand_ref[r, block] for r in range(RANDOMS)]
        biases = [
            bias(block - 1, block >= 1),
            bias(block, block >= 0),
            bias(block + 1, block + 1 < blocks),
        ]
        query = qs[h, slot]
        slots = [lax.rem(i, ranks) * GROUPS + lax.div(i, ranks) for i in ids]
        key = jnp.concatenate([kvs[h][i, 0] for i in slots], axis=0)
        value = jnp.concatenate([kvs[h][i, 1] for i in slots], axis=0)
        scores = lax.dot_general(
            query, key, (((1,), (1,)), ((), ())), preferred_element_type=jnp.float32
        ) * (HEAD_DIM ** -0.5)
        parts = [scores[:, n * BLOCK : (n + 1) * BLOCK] for n in range(len(ids))]
        parts = [part + biases[n] if n < 3 else part for n, part in enumerate(parts)]
        top = jnp.max(functools.reduce(jnp.maximum, parts), axis=1, keepdims=True)
        powers = [jnp.exp(part - top) for part in parts]
        total = jnp.sum(functools.reduce(jnp.add, powers), axis=1, keepdims=True)
        inverse = 1.0 / total
        probs = jnp.concatenate([(power * inverse).astype(jnp.bfloat16) for power in powers], axis=1)
        result = lax.dot_general(
            probs, value, (((1,), (0,)), ((), ())), preferred_element_type=jnp.float32
        )
        os[h, slot] = result.astype(jnp.bfloat16)

    upper = group >= GROUPS // 2
    inner = (group >= GROUPS // 4) & (group < GROUPS - GROUPS // 4)
    last = LOCAL_HEADS - 1

    for h in range(LOCAL_HEADS):
        wait_bytes(mine(h), kv_recv.at[h])

        @pl.loop(1, ranks)
        def _(i):
            forward(h, i)

        wait_bytes(qs.at[h], q_recv.at[h])
        wait_bytes(kvs[h].at[pl.ds(0, (ranks - 1) * GROUPS)], fwd_recv.at[h])

        if h == last:
            @pl.when(jnp.logical_not(inner))
            def _():
                for earlier in range(last):
                    @pl.loop(0, GROUPS // 2)
                    def _(k):
                        send_out(earlier, k + jnp.where(upper, 0, GROUPS // 2))

        def attend_and_send(p):
            attend(h, p)
            now = p != group
            if h < last:
                now &= inner | ((p >= GROUPS // 2) == upper)
            if h == last - 1:
                held = functools.reduce(jnp.logical_or, [p == q for q in HELD])
                now &= jnp.logical_not(inner & upper & held)

            @pl.when(now)
            def _():
                send_out(h, p)

            if h == last:
                @pl.when(inner & upper & (p == 1))
                def _():
                    for q in HELD:
                        send_out(h - 1, q)

        in_order(RESULTS, attend_and_send)
        out_local(h)

    sent = os.at[:, pl.ds(0, GROUPS - 1)]
    for t in (1, 2, 0):
        wait_bytes(sent, send_sem.at[t])

    @pl.loop(1, ranks)
    def _(i):
        for h in range(LOCAL_HEADS):
            wait_bytes(mine(h), fwd_send.at[h, i - 1])

    wait_bytes(sent, out_send)
    wait_bytes(out_hbm, out_recv)


def local(queries, keys, values, rand_blocks, global_ids):
    seq = lax.axis_size("seq")
    ranks = seq // GROUPS
    blocks = rand_blocks.shape[0]
    assert queries.shape[0] == BLOCK and blocks == seq and seq % GROUPS == 0
    tile = (BLOCK, HEAD_DIM)
    sources = [pltpu.with_memory_space_constraint(x, pltpu.MemorySpace.HBM) for x in (rand_blocks.T, global_ids, queries, keys, values)]
    anywhere = pl.BlockSpec(memory_space=pl.ANY)
    dma = pltpu.SemaphoreType.DMA
    return pl.pallas_call(
        functools.partial(kernel, ranks),
        out_shape=jax.ShapeDtypeStruct(queries.shape, jnp.bfloat16),
        in_specs=[anywhere] * 5,
        out_specs=anywhere,
        scratch_shapes=[
            pltpu.VMEM((LOCAL_HEADS, GROUPS) + tile, jnp.bfloat16),
            pltpu.VMEM((LOCAL_HEADS, GROUPS) + tile, jnp.bfloat16),
            pltpu.SMEM((RANDOMS, blocks), jnp.int32),
            pltpu.SMEM((GLOBALS,), jnp.int32),
        ]
        + [pltpu.VMEM((blocks, 2) + tile, jnp.bfloat16)] * LOCAL_HEADS
        + [
            dma((2,)),
            dma((3,)),
            dma((LOCAL_HEADS,)),
            dma((LOCAL_HEADS,)),
            dma((LOCAL_HEADS, ranks - 1)),
            dma((LOCAL_HEADS,)),
            dma,
            dma,
            pltpu.SemaphoreType.REGULAR((GROUPS // 2,)),
        ],
        compiler_params=pltpu.CompilerParams(
            collective_id=0, has_side_effects=True, vmem_limit_bytes=40 << 20
        ),
    )(*sources)


def solution(mesh):
    placed = (
        P(("groups", "seq"), None),
        P(("groups", "seq"), None),
        P(("groups", "seq"), None),
        P("groups", None),
        P("groups"),
    )
    return jax.shard_map(
        local, mesh=mesh, in_specs=placed, out_specs=P(("groups", "seq"), None), check_vma=False
    )
```

```python
import functools

import jax
import jax.numpy as jnp
from jax import lax
from jax.experimental import pallas as pl
from jax.experimental.pallas import tpu as pltpu
from jax.sharding import PartitionSpec as P

HEADS = 24
HEAD_DIM = 128
BLOCK = 128
GLOBALS = 2
RANDOMS = 3
LOCAL_HEADS = 3
GROUPS = HEADS // LOCAL_HEADS
MESH = pl.DeviceIdType.MESH
NEG = -1e30


SENDS = (
    (6, 7, 4, 5, 2, 3, 1, 0),
    (7, 6, 4, 5, 3, 2, 0, 1),
    (6, 7, 4, 5, 0, 1, 3, 2),
    (6, 7, 4, 5, 0, 1, 2, 3),
    (0, 1, 2, 3, 6, 7, 5, 4),
    (0, 1, 2, 3, 6, 7, 4, 5),
    (0, 1, 2, 3, 4, 5, 7, 6),
    (0, 1, 2, 3, 4, 5, 6, 7),
)
RESULTS = (
    (4, 6, 5, 7, 2, 1, 3, 0),
    (4, 6, 5, 7, 0, 2, 3, 1),
    (0, 1, 4, 6, 7, 5, 3, 2),
    (0, 2, 1, 4, 6, 5, 7, 3),
    (0, 1, 2, 3, 6, 7, 5, 4),
    (0, 1, 2, 3, 6, 7, 4, 5),
    (0, 1, 2, 3, 4, 5, 7, 6),
    (0, 1, 2, 3, 4, 5, 6, 7),
)
HELD = (1, 2, 3)
SIGNALS = (
    (5, 4, 3, 2, 1, 7, 6),
    (0, 2, 3, 5, 6, 7),
    (4, 5, 3, 6, 7),
    (5, 6, 7),
    (2, 5, 3, 1, 6, 7),
    (3, 6, 7),
    (7,),
    (6,),
)
HEARD = ((1,), (4, 0), (4, 0, 1), (5, 4, 2, 0, 1), (2, 0), (3, 2, 1, 0, 4), (0, 1, 2, 3, 4, 5, 7), (0, 1, 2, 3, 4, 5, 6))
LATER = ((4, 2, 5, 3, 7, 6), (2, 5, 3, 7, 6), (5, 3, 7, 6), (7, 6), (5, 3, 1, 7, 6), (7, 6), (), ())
TELLS = tuple(tuple(q for q in range(GROUPS) if p in LATER[q]) for p in range(GROUPS))


def kernel(ranks, rand_hbm, glob_hbm, q_hbm, k_hbm, v_hbm, out_hbm, qs, os, rand_ref, glob_ref, *scratch):
    kvs = scratch[:LOCAL_HEADS]
    (table_sem, send_sem, q_recv, kv_recv, fwd_send, fwd_recv, out_send, out_recv, ready, sibling_ready) = scratch[LOCAL_HEADS:]
    rollout = lax.axis_index("groups")
    me = lax.axis_index("seq")
    group, rank = lax.div(me, ranks), lax.rem(me, ranks)
    blocks = ranks * GROUPS
    def sibling(i):
        return group * ranks + lax.rem(rank + i, ranks)

    def device(index):
        return (rollout, index)

    def pick(values):
        return functools.reduce(lambda rest, g: jnp.where(group == g, values[g], rest), range(1, GROUPS), values[0])

    def in_order(rows, body):
        code = pick([sum(p << 3 * k for k, p in enumerate(row)) for row in rows])

        @pl.loop(0, pick([len(row) for row in rows]))
        def _(k):
            body(lax.shift_right_logical(code, 3 * k) & 7)

    barrier = pltpu.get_barrier_semaphore()

    def signal(semaphore, index):
        pl.semaphore_signal(semaphore, inc=1, device_id=device(index), device_id_type=MESH)

    in_order(SIGNALS, lambda p: signal(barrier, p * ranks + rank))

    @pl.loop(0, rank)
    def _(i):
        signal(barrier, group * ranks + i)

    tables = (
        pltpu.make_async_copy(rand_hbm, rand_ref, table_sem.at[0]),
        pltpu.make_async_copy(glob_hbm, glob_ref, table_sem.at[1]),
    )
    for table in tables:
        table.start()

    sources = (q_hbm, k_hbm, v_hbm)

    def columns(owner, h):
        start = pl.multiple_of((owner * LOCAL_HEADS + h) * HEAD_DIM, HEAD_DIM)
        return pl.ds(start, HEAD_DIM)

    def slab(t, h, owner_group):
        if t == 0:
            return qs.at[h, owner_group]
        return kvs[h].at[rank * GROUPS + owner_group, t - 1]

    def send(h, p, which=(1, 2, 0)):
        for t in which:
            pltpu.make_async_remote_copy(
                src_ref=sources[t].at[:, columns(p, h)],
                dst_ref=slab(t, h, group),
                send_sem=send_sem.at[t],
                recv_sem=(q_recv if t == 0 else kv_recv).at[h],
                device_id=device(p * ranks + rank),
                device_id_type=MESH,
            ).start()

    def own(h):
        for t in (1, 2, 0):
            pltpu.make_async_copy(
                sources[t].at[:, columns(group, h)], slab(t, h, group), (q_recv if t == 0 else kv_recv).at[h]
            ).start()

    def mine(h):
        return kvs[h].at[pl.ds(rank * GROUPS, GROUPS)]

    def forward(h, i):
        pltpu.make_async_remote_copy(
            src_ref=mine(h),
            dst_ref=mine(h),
            send_sem=fwd_send.at[h, i - 1],
            recv_sem=fwd_recv.at[h],
            device_id=device(sibling(i)),
            device_id_type=MESH,
        ).start()

    def send_out(h, p):
        pltpu.make_async_remote_copy(
            src_ref=os.at[h, p],
            dst_ref=out_hbm.at[:, columns(group, h)],
            send_sem=out_send,
            recv_sem=out_recv,
            device_id=device(p * ranks + rank),
            device_id_type=MESH,
        ).start()

    def out_local(h):
        pltpu.make_async_copy(os.at[h, group], out_hbm.at[:, columns(group, h)], out_recv).start()

    def wait_bytes(ref, sem):
        pltpu.make_async_copy(ref, ref, sem).wait()

    pl.semaphore_wait(barrier, pick([len(row) for row in HEARD]) + ranks - 1 - rank)

    in_order(TELLS, lambda p: signal(ready.at[group], p * ranks + rank))
    in_order(HEARD, lambda p: send(0, p))

    @pl.loop(rank + 1, ranks)
    def _(i):
        signal(sibling_ready, group * ranks + i)

    own(0)

    def send_later(p):
        pl.semaphore_wait(ready.at[p], 1)
        send(0, p)

    in_order(LATER, send_later)

    for h, which in ((1, (1, 2, 0)), (2, (1, 2)), (2, (0,))):
        def send_others(p):
            @pl.when(p != group)
            def _():
                send(h, p, which)

        in_order(SENDS, send_others)
        if 0 in which:
            own(h)

    for table in tables:
        table.wait()

    @pl.when(rank > 0)
    def _():
        pl.semaphore_wait(sibling_ready, rank)

    def attend(h, slot):
        block = slot * ranks + rank
        g0, g1 = glob_ref[0], glob_ref[1]

        def bias(b, inside):
            ok = inside & (b != g0) & (b != g1)
            return jnp.where(ok, jnp.float32(0.0), jnp.float32(NEG))

        ids = [
            jnp.maximum(block - 1, 0),
            block,
            jnp.minimum(block + 1, blocks - 1),
            g0,
            g1,
        ] + [rand_ref[r, block] for r in range(RANDOMS)]
        biases = [
            bias(block - 1, block >= 1),
            bias(block, block >= 0),
            bias(block + 1, block + 1 < blocks),
        ]
        query = qs[h, slot]
        slots = [lax.rem(i, ranks) * GROUPS + lax.div(i, ranks) for i in ids]
        key = jnp.concatenate([kvs[h][i, 0] for i in slots], axis=0)
        value = jnp.concatenate([kvs[h][i, 1] for i in slots], axis=0)
        scores = lax.dot_general(
            query, key, (((1,), (1,)), ((), ())), preferred_element_type=jnp.float32
        ) * (HEAD_DIM ** -0.5)
        parts = [scores[:, n * BLOCK : (n + 1) * BLOCK] for n in range(len(ids))]
        parts = [part + biases[n] if n < 3 else part for n, part in enumerate(parts)]
        top = jnp.max(functools.reduce(jnp.maximum, parts), axis=1, keepdims=True)
        powers = [jnp.exp(part - top) for part in parts]
        total = jnp.sum(functools.reduce(jnp.add, powers), axis=1, keepdims=True)
        inverse = 1.0 / total
        probs = jnp.concatenate([(power * inverse).astype(jnp.bfloat16) for power in powers], axis=1)
        result = lax.dot_general(
            probs, value, (((1,), (0,)), ((), ())), preferred_element_type=jnp.float32
        )
        os[h, slot] = result.astype(jnp.bfloat16)

    upper = group >= GROUPS // 2
    inner = (group >= GROUPS // 4) & (group < GROUPS - GROUPS // 4)
    last = LOCAL_HEADS - 1

    for h in range(LOCAL_HEADS):
        wait_bytes(mine(h), kv_recv.at[h])

        @pl.loop(1, ranks)
        def _(i):
            forward(h, i)

        wait_bytes(qs.at[h], q_recv.at[h])
        wait_bytes(kvs[h].at[pl.ds(0, (ranks - 1) * GROUPS)], fwd_recv.at[h])

        if h == last:
            @pl.when(jnp.logical_not(inner))
            def _():
                for earlier in range(last):
                    @pl.loop(0, GROUPS // 2)
                    def _(k):
                        send_out(earlier, k + jnp.where(upper, 0, GROUPS // 2))

        def attend_and_send(p):
            attend(h, p)
            now = p != group
            if h < last:
                now &= inner | ((p >= GROUPS // 2) == upper)
            if h == last - 1:
                held = functools.reduce(jnp.logical_or, [p == q for q in HELD])
                now &= jnp.logical_not(inner & upper & held)

            @pl.when(now)
            def _():
                send_out(h, p)

            if h == last:
                @pl.when(inner & upper & (p == 0))
                def _():
                    for q in HELD:
                        send_out(h - 1, q)

        in_order(RESULTS, attend_and_send)
        out_local(h)

    sent = os.at[:, pl.ds(0, GROUPS - 1)]
    for t in (1, 2, 0):
        wait_bytes(sent, send_sem.at[t])

    @pl.loop(1, ranks)
    def _(i):
        for h in range(LOCAL_HEADS):
            wait_bytes(mine(h), fwd_send.at[h, i - 1])

    wait_bytes(sent, out_send)
    wait_bytes(out_hbm, out_recv)


def local(queries, keys, values, rand_blocks, global_ids):
    seq = lax.axis_size("seq")
    ranks = seq // GROUPS
    blocks = rand_blocks.shape[0]
    assert queries.shape[0] == BLOCK and blocks == seq and seq % GROUPS == 0
    tile = (BLOCK, HEAD_DIM)
    sources = [pltpu.with_memory_space_constraint(x, pltpu.MemorySpace.HBM) for x in (rand_blocks.T, global_ids, queries, keys, values)]
    anywhere = pl.BlockSpec(memory_space=pl.ANY)
    dma = pltpu.SemaphoreType.DMA
    return pl.pallas_call(
        functools.partial(kernel, ranks),
        out_shape=jax.ShapeDtypeStruct(queries.shape, jnp.bfloat16),
        in_specs=[anywhere] * 5,
        out_specs=anywhere,
        scratch_shapes=[
            pltpu.VMEM((LOCAL_HEADS, GROUPS) + tile, jnp.bfloat16),
            pltpu.VMEM((LOCAL_HEADS, GROUPS) + tile, jnp.bfloat16),
            pltpu.SMEM((RANDOMS, blocks), jnp.int32),
            pltpu.SMEM((GLOBALS,), jnp.int32),
        ]
        + [pltpu.VMEM((blocks, 2) + tile, jnp.bfloat16)] * LOCAL_HEADS
        + [
            dma((2,)),
            dma((3,)),
            dma((LOCAL_HEADS,)),
            dma((LOCAL_HEADS,)),
            dma((LOCAL_HEADS, ranks - 1)),
            dma((LOCAL_HEADS,)),
            dma,
            dma,
            pltpu.SemaphoreType.REGULAR((GROUPS,)),
            pltpu.SemaphoreType.REGULAR,
        ],
        compiler_params=pltpu.CompilerParams(
            collective_id=0, has_side_effects=True, vmem_limit_bytes=40 << 20
        ),
    )(*sources)


def solution(mesh):
    placed = (
        P(("groups", "seq"), None),
        P(("groups", "seq"), None),
        P(("groups", "seq"), None),
        P("groups", None),
        P("groups"),
    )
    return jax.shard_map(
        local, mesh=mesh, in_specs=placed, out_specs=P(("groups", "seq"), None), check_vma=False
    )
```

```python
import functools

import jax
import jax.numpy as jnp
from jax import lax
from jax.experimental import pallas as pl
from jax.experimental.pallas import tpu as pltpu
from jax.sharding import PartitionSpec as P

HEADS = 24
HEAD_DIM = 128
BLOCK = 128
GLOBALS = 2
RANDOMS = 3
LOCAL_HEADS = 3
GROUPS = HEADS // LOCAL_HEADS
MESH = pl.DeviceIdType.MESH
NEG = -1e30


SENDS = (
    (6, 7, 4, 5, 2, 3, 1, 0),
    (7, 6, 4, 5, 3, 2, 0, 1),
    (6, 7, 4, 5, 0, 1, 3, 2),
    (6, 7, 4, 5, 0, 1, 2, 3),
    (0, 1, 2, 3, 6, 7, 5, 4),
    (0, 1, 2, 3, 6, 7, 4, 5),
    (0, 1, 2, 3, 4, 5, 7, 6),
    (0, 1, 2, 3, 4, 5, 6, 7),
)
LAST_SENDS = (
    (4, 5, 6, 7, 2, 3, 1, 0),
    (5, 4, 7, 6, 3, 2, 0, 1),
    (4, 5, 6, 7, 0, 1, 3, 2),
    (5, 4, 7, 6, 0, 1, 2, 3),
    (2, 3, 0, 1, 6, 7, 5, 4),
    (3, 2, 1, 0, 6, 7, 4, 5),
    (2, 3, 0, 1, 4, 5, 7, 6),
    (3, 2, 1, 0, 4, 5, 6, 7),
)
RESULTS = (
    (4, 6, 5, 7, 2, 1, 3, 0),
    (4, 6, 5, 7, 0, 2, 3, 1),
    (0, 1, 4, 6, 7, 5, 3, 2),
    (0, 2, 1, 4, 6, 5, 7, 3),
    (0, 1, 2, 3, 6, 7, 5, 4),
    (0, 1, 2, 3, 4, 6, 7, 5),
    (0, 1, 2, 3, 4, 5, 7, 6),
    (0, 1, 2, 3, 4, 5, 6, 7),
)
HELD = {1: (1,), 2: (1,), 3: (0, 1)}
RELEASED = {0: ((1, 1), (1, 2)), 2: ((0, 3), (1, 3))}
SIGNALS = (
    (5, 4, 3, 2, 1, 7, 6),
    (0, 2, 3, 5, 6, 7),
    (4, 5, 3, 6, 7),
    (5, 6, 7),
    (2, 5, 3, 1, 6, 7),
    (3, 6, 7),
    (7,),
    (6,),
)
HEARD = ((1,), (4, 0), (4, 0, 1), (5, 4, 2, 0, 1), (2, 0), (3, 2, 1, 0, 4), (0, 1, 2, 3, 4, 5, 7), (0, 1, 2, 3, 4, 5, 6))
LATER = ((4, 2, 5, 3, 7, 6), (2, 5, 3, 7, 6), (5, 3, 7, 6), (7, 6), (5, 3, 1, 7, 6), (7, 6), (), ())
TELLS = tuple(tuple(q for q in range(GROUPS) if p in LATER[q]) for p in range(GROUPS))


def kernel(ranks, rand_hbm, glob_hbm, q_hbm, k_hbm, v_hbm, out_hbm, qs, os, rand_ref, glob_ref, *scratch):
    kvs = scratch[:LOCAL_HEADS]
    (table_sem, send_sem, q_recv, kv_recv, fwd_send, fwd_recv, out_send, out_recv, ready, sibling_ready) = scratch[LOCAL_HEADS:]
    rollout = lax.axis_index("groups")
    me = lax.axis_index("seq")
    group, rank = lax.div(me, ranks), lax.rem(me, ranks)
    blocks = ranks * GROUPS
    def sibling(i):
        return group * ranks + lax.rem(rank + i, ranks)

    def device(index):
        return (rollout, index)

    def pick(values):
        return functools.reduce(lambda rest, g: jnp.where(group == g, values[g], rest), range(1, GROUPS), values[0])

    def in_order(rows, body):
        code = pick([sum(p << 3 * k for k, p in enumerate(row)) for row in rows])

        @pl.loop(0, pick([len(row) for row in rows]))
        def _(k):
            body(lax.shift_right_logical(code, 3 * k) & 7)

    barrier = pltpu.get_barrier_semaphore()

    def signal(semaphore, index):
        pl.semaphore_signal(semaphore, inc=1, device_id=device(index), device_id_type=MESH)

    in_order(SIGNALS, lambda p: signal(barrier, p * ranks + rank))

    @pl.loop(0, rank)
    def _(i):
        signal(barrier, group * ranks + i)

    tables = (
        pltpu.make_async_copy(rand_hbm, rand_ref, table_sem.at[0]),
        pltpu.make_async_copy(glob_hbm, glob_ref, table_sem.at[1]),
    )
    for table in tables:
        table.start()

    sources = (q_hbm, k_hbm, v_hbm)

    def columns(owner, h):
        start = pl.multiple_of((owner * LOCAL_HEADS + h) * HEAD_DIM, HEAD_DIM)
        return pl.ds(start, HEAD_DIM)

    def slab(t, h, owner_group):
        if t == 0:
            return qs.at[h, owner_group]
        return kvs[h].at[rank * GROUPS + owner_group, t - 1]

    def send(h, p, which=(1, 2, 0)):
        for t in which:
            pltpu.make_async_remote_copy(
                src_ref=sources[t].at[:, columns(p, h)],
                dst_ref=slab(t, h, group),
                send_sem=send_sem.at[t],
                recv_sem=(q_recv if t == 0 else kv_recv).at[h],
                device_id=device(p * ranks + rank),
                device_id_type=MESH,
            ).start()

    def own(h):
        for t in (1, 2, 0):
            pltpu.make_async_copy(
                sources[t].at[:, columns(group, h)], slab(t, h, group), (q_recv if t == 0 else kv_recv).at[h]
            ).start()

    def mine(h):
        return kvs[h].at[pl.ds(rank * GROUPS, GROUPS)]

    def forward(h, i):
        pltpu.make_async_remote_copy(
            src_ref=mine(h),
            dst_ref=mine(h),
            send_sem=fwd_send.at[h, i - 1],
            recv_sem=fwd_recv.at[h],
            device_id=device(sibling(i)),
            device_id_type=MESH,
        ).start()

    def send_out(h, p):
        pltpu.make_async_remote_copy(
            src_ref=os.at[h, p],
            dst_ref=out_hbm.at[:, columns(group, h)],
            send_sem=out_send,
            recv_sem=out_recv,
            device_id=device(p * ranks + rank),
            device_id_type=MESH,
        ).start()

    def out_local(h):
        pltpu.make_async_copy(os.at[h, group], out_hbm.at[:, columns(group, h)], out_recv).start()

    def wait_bytes(ref, sem):
        pltpu.make_async_copy(ref, ref, sem).wait()

    pl.semaphore_wait(barrier, pick([len(row) for row in HEARD]) + ranks - 1 - rank)

    in_order(TELLS, lambda p: signal(ready.at[group], p * ranks + rank))
    in_order(HEARD, lambda p: send(0, p))

    @pl.loop(rank + 1, ranks)
    def _(i):
        signal(sibling_ready, group * ranks + i)

    own(0)

    def send_later(p):
        pl.semaphore_wait(ready.at[p], 1)
        send(0, p)

    in_order(LATER, send_later)

    for h, which in ((1, (1, 2, 0)), (2, (1, 2)), (2, (0,))):
        def send_others(p):
            @pl.when(p != group)
            def _():
                send(h, p, which)

        in_order(LAST_SENDS if h == LOCAL_HEADS - 1 else SENDS, send_others)
        if 0 in which:
            own(h)

    for table in tables:
        table.wait()

    @pl.when(rank > 0)
    def _():
        pl.semaphore_wait(sibling_ready, rank)

    def attend(h, slot):
        block = slot * ranks + rank
        g0, g1 = glob_ref[0], glob_ref[1]

        def bias(b, inside):
            ok = inside & (b != g0) & (b != g1)
            return jnp.where(ok, jnp.float32(0.0), jnp.float32(NEG))

        ids = [
            jnp.maximum(block - 1, 0),
            block,
            jnp.minimum(block + 1, blocks - 1),
            g0,
            g1,
        ] + [rand_ref[r, block] for r in range(RANDOMS)]
        biases = [
            bias(block - 1, block >= 1),
            bias(block, block >= 0),
            bias(block + 1, block + 1 < blocks),
        ]
        query = qs[h, slot]
        slots = [lax.rem(i, ranks) * GROUPS + lax.div(i, ranks) for i in ids]
        key = jnp.concatenate([kvs[h][i, 0] for i in slots], axis=0)
        value = jnp.concatenate([kvs[h][i, 1] for i in slots], axis=0)
        scores = lax.dot_general(
            query, key, (((1,), (1,)), ((), ())), preferred_element_type=jnp.float32
        ) * (HEAD_DIM ** -0.5)
        parts = [scores[:, n * BLOCK : (n + 1) * BLOCK] for n in range(len(ids))]
        parts = [part + biases[n] if n < 3 else part for n, part in enumerate(parts)]
        top = jnp.max(functools.reduce(jnp.maximum, parts), axis=1, keepdims=True)
        powers = [jnp.exp(part - top) for part in parts]
        total = jnp.sum(functools.reduce(jnp.add, powers), axis=1, keepdims=True)
        inverse = 1.0 / total
        probs = jnp.concatenate([(power * inverse).astype(jnp.bfloat16) for power in powers], axis=1)
        result = lax.dot_general(
            probs, value, (((1,), (0,)), ((), ())), preferred_element_type=jnp.float32
        )
        os[h, slot] = result.astype(jnp.bfloat16)

    upper = group >= GROUPS // 2
    inner = (group >= GROUPS // 4) & (group < GROUPS - GROUPS // 4)
    last = LOCAL_HEADS - 1

    for h in range(LOCAL_HEADS):
        wait_bytes(mine(h), kv_recv.at[h])

        @pl.loop(1, ranks)
        def _(i):
            forward(h, i)

        wait_bytes(qs.at[h], q_recv.at[h])
        wait_bytes(kvs[h].at[pl.ds(0, (ranks - 1) * GROUPS)], fwd_recv.at[h])

        if h == last:
            @pl.when(jnp.logical_not(inner))
            def _():
                for earlier in range(last):
                    @pl.loop(0, GROUPS // 2)
                    def _(k):
                        send_out(earlier, k + jnp.where(upper, 0, GROUPS // 2))

        def attend_and_send(p):
            attend(h, p)
            now = p != group
            if h < last:
                now &= inner | ((p >= GROUPS // 2) == upper)
            held = [q for q, heads in HELD.items() if h in heads]
            if held:
                now &= jnp.logical_not(inner & upper & functools.reduce(jnp.logical_or, [p == q for q in held]))

            @pl.when(now)
            def _():
                send_out(h, p)

            if h == last:
                for trigger, results in RELEASED.items():
                    @pl.when(inner & upper & (p == trigger))
                    def _():
                        for earlier, q in results:
                            send_out(earlier, q)

        in_order(RESULTS, attend_and_send)
        out_local(h)

    sent = os.at[:, pl.ds(0, GROUPS - 1)]
    for t in (1, 2, 0):
        wait_bytes(sent, send_sem.at[t])

    @pl.loop(1, ranks)
    def _(i):
        for h in range(LOCAL_HEADS):
            wait_bytes(mine(h), fwd_send.at[h, i - 1])

    wait_bytes(sent, out_send)
    wait_bytes(out_hbm, out_recv)


def local(queries, keys, values, rand_blocks, global_ids):
    seq = lax.axis_size("seq")
    ranks = seq // GROUPS
    blocks = rand_blocks.shape[0]
    assert queries.shape[0] == BLOCK and blocks == seq and seq % GROUPS == 0
    tile = (BLOCK, HEAD_DIM)
    sources = [pltpu.with_memory_space_constraint(x, pltpu.MemorySpace.HBM) for x in (rand_blocks.T, global_ids, queries, keys, values)]
    anywhere = pl.BlockSpec(memory_space=pl.ANY)
    dma = pltpu.SemaphoreType.DMA
    return pl.pallas_call(
        functools.partial(kernel, ranks),
        out_shape=jax.ShapeDtypeStruct(queries.shape, jnp.bfloat16),
        in_specs=[anywhere] * 5,
        out_specs=anywhere,
        scratch_shapes=[
            pltpu.VMEM((LOCAL_HEADS, GROUPS) + tile, jnp.bfloat16),
            pltpu.VMEM((LOCAL_HEADS, GROUPS) + tile, jnp.bfloat16),
            pltpu.SMEM((RANDOMS, blocks), jnp.int32),
            pltpu.SMEM((GLOBALS,), jnp.int32),
        ]
        + [pltpu.VMEM((blocks, 2) + tile, jnp.bfloat16)] * LOCAL_HEADS
        + [
            dma((2,)),
            dma((3,)),
            dma((LOCAL_HEADS,)),
            dma((LOCAL_HEADS,)),
            dma((LOCAL_HEADS, ranks - 1)),
            dma((LOCAL_HEADS,)),
            dma,
            dma,
            pltpu.SemaphoreType.REGULAR((GROUPS,)),
            pltpu.SemaphoreType.REGULAR,
        ],
        compiler_params=pltpu.CompilerParams(
            collective_id=0, has_side_effects=True, vmem_limit_bytes=40 << 20
        ),
    )(*sources)


def solution(mesh):
    placed = (
        P(("groups", "seq"), None),
        P(("groups", "seq"), None),
        P(("groups", "seq"), None),
        P("groups", None),
        P("groups"),
    )
    return jax.shard_map(
        local, mesh=mesh, in_specs=placed, out_specs=P(("groups", "seq"), None), check_vma=False
    )
```

```python
import functools

import jax
import jax.numpy as jnp
from jax import lax
from jax.experimental import pallas as pl
from jax.experimental.pallas import tpu as pltpu
from jax.sharding import PartitionSpec as P

HEADS = 24
HEAD_DIM = 128
BLOCK = 128
GLOBALS = 2
RANDOMS = 3
LOCAL_HEADS = 3
GROUPS = HEADS // LOCAL_HEADS
MESH = pl.DeviceIdType.MESH
NEG = -1e30


SENDS = (
    (6, 7, 4, 5, 2, 3, 1, 0),
    (7, 6, 4, 5, 3, 2, 0, 1),
    (6, 7, 4, 5, 0, 1, 3, 2),
    (6, 7, 4, 5, 0, 1, 2, 3),
    (0, 1, 2, 3, 6, 7, 5, 4),
    (0, 1, 2, 3, 6, 7, 4, 5),
    (0, 1, 2, 3, 4, 5, 7, 6),
    (0, 1, 2, 3, 4, 5, 6, 7),
)
LAST_SENDS = (
    (5, 4, 7, 6, 2, 3, 1, 0),
    (5, 4, 7, 6, 3, 2, 0, 1),
    (5, 4, 7, 6, 0, 1, 3, 2),
    (5, 4, 7, 6, 0, 1, 2, 3),
    (3, 2, 1, 0, 6, 7, 5, 4),
    (3, 2, 1, 0, 6, 7, 4, 5),
    (3, 2, 1, 0, 4, 5, 7, 6),
    (3, 2, 1, 0, 4, 5, 6, 7),
)
RESULTS = (
    (4, 6, 5, 7, 2, 1, 3, 0),
    (4, 6, 5, 7, 0, 2, 3, 1),
    (0, 1, 4, 6, 7, 5, 3, 2),
    (0, 2, 1, 4, 6, 5, 7, 3),
    (0, 1, 3, 2, 6, 7, 5, 4),
    (0, 1, 2, 3, 4, 6, 7, 5),
    (0, 1, 2, 3, 4, 5, 7, 6),
    (0, 1, 2, 3, 4, 5, 6, 7),
)
HELD = {1: (1,), 2: (1,), 3: (0, 1)}
RELEASED = {0: ((1, 1), (1, 2)), 2: ((0, 3), (1, 3))}
SIGNALS = (
    (5, 4, 3, 2, 1, 7, 6),
    (0, 2, 3, 5, 6, 7),
    (4, 5, 3, 6, 7),
    (5, 6, 7),
    (2, 3, 1, 6, 7),
    (3, 6, 7),
    (7,),
    (6,),
)
HEARD = ((1,), (4, 0), (4, 0, 1), (5, 4, 2, 0, 1), (2, 0), (3, 2, 1, 0), (0, 1, 2, 3, 4, 5, 7), (0, 1, 2, 3, 4, 5, 6))
LATER = ((4, 2, 5, 3, 7, 6), (2, 5, 3, 7, 6), (5, 3, 7, 6), (7, 6), (3, 5, 1, 7, 6), (4, 7, 6), (), ())
TELLS = ((), (4,), (0, 1), (5, 0, 1, 2, 4), (0,), (0, 1, 2), (0, 1, 2, 3, 4, 5), (0, 1, 2, 3, 4, 5))


def kernel(ranks, rand_hbm, glob_hbm, q_hbm, k_hbm, v_hbm, out_hbm, qs, os, rand_ref, glob_ref, *scratch):
    kvs = scratch[:LOCAL_HEADS]
    (send_sem, q_recv, kv_recv, fwd_send, fwd_recv, out_send, out_recv, ready, sibling_ready) = scratch[LOCAL_HEADS:]
    rollout = lax.axis_index("groups")
    me = lax.axis_index("seq")
    group, rank = lax.div(me, ranks), lax.rem(me, ranks)
    blocks = ranks * GROUPS
    def sibling(i):
        return group * ranks + lax.rem(rank + i, ranks)

    def device(index):
        return (rollout, index)

    def pick(values):
        return functools.reduce(lambda rest, g: jnp.where(group == g, values[g], rest), range(1, GROUPS), values[0])

    def in_order(rows, body):
        code = pick([sum(p << 3 * k for k, p in enumerate(row)) for row in rows])

        @pl.loop(0, pick([len(row) for row in rows]))
        def _(k):
            body(lax.shift_right_logical(code, 3 * k) & 7)

    barrier = pltpu.get_barrier_semaphore()

    def signal(semaphore, index):
        pl.semaphore_signal(semaphore, inc=1, device_id=device(index), device_id_type=MESH)

    in_order(SIGNALS, lambda p: signal(barrier, p * ranks + rank))

    @pl.loop(0, rank)
    def _(i):
        signal(barrier, group * ranks + i)

    tables = (
        pltpu.make_async_copy(rand_hbm, rand_ref, fwd_send.at[0]),
        pltpu.make_async_copy(glob_hbm, glob_ref, out_send),
    )
    for table in tables:
        table.start()

    sources = (q_hbm, k_hbm, v_hbm)

    def columns(owner, h):
        start = pl.multiple_of((owner * LOCAL_HEADS + h) * HEAD_DIM, HEAD_DIM)
        return pl.ds(start, HEAD_DIM)

    def slab(t, h, owner_group):
        if t == 0:
            return qs.at[h, owner_group]
        return kvs[h].at[rank * GROUPS + owner_group, t - 1]

    def send(h, p, which=(1, 2, 0)):
        for t in which:
            pltpu.make_async_remote_copy(
                src_ref=sources[t].at[:, columns(p, h)],
                dst_ref=slab(t, h, group),
                send_sem=send_sem.at[t],
                recv_sem=(q_recv if t == 0 else kv_recv).at[h],
                device_id=device(p * ranks + rank),
                device_id_type=MESH,
            ).start()

    def own(h):
        for t in (1, 2, 0):
            pltpu.make_async_copy(
                sources[t].at[:, columns(group, h)], slab(t, h, group), (q_recv if t == 0 else kv_recv).at[h]
            ).start()

    def mine(h):
        return kvs[h].at[pl.ds(rank * GROUPS, GROUPS)]

    def forward(h, i):
        pltpu.make_async_remote_copy(
            src_ref=mine(h),
            dst_ref=mine(h),
            send_sem=fwd_send.at[i - 1],
            recv_sem=fwd_recv.at[h],
            device_id=device(sibling(i)),
            device_id_type=MESH,
        ).start()

    def send_out(h, p):
        pltpu.make_async_remote_copy(
            src_ref=os.at[h, p],
            dst_ref=out_hbm.at[:, columns(group, h)],
            send_sem=out_send,
            recv_sem=out_recv,
            device_id=device(p * ranks + rank),
            device_id_type=MESH,
        ).start()

    def out_local(h):
        pltpu.make_async_copy(os.at[h, group], out_hbm.at[:, columns(group, h)], out_recv).start()

    def wait_bytes(ref, sem):
        pltpu.make_async_copy(ref, ref, sem).wait()

    pl.semaphore_wait(barrier, pick([len(row) for row in HEARD]) + ranks - 1 - rank)

    in_order(TELLS, lambda p: signal(ready.at[jnp.minimum(group, GROUPS - 2)], p * ranks + rank))
    in_order(HEARD, lambda p: send(0, p))

    @pl.loop(rank + 1, ranks)
    def _(i):
        signal(sibling_ready, group * ranks + i)

    own(0)

    def send_later(p):
        @pl.when((p < GROUPS - 2) & jnp.logical_not((group == 4) & (p == 5)))
        def _():
            pl.semaphore_wait(ready.at[jnp.where((group == 5) & (p == 4), 3, p)], 1)

        @pl.when(p == GROUPS - 1)
        def _():
            pl.semaphore_wait(ready.at[GROUPS - 2], 2)

        send(0, p)

    in_order(LATER, send_later)

    for h, which in ((1, (1, 2, 0)), (2, (1, 2)), (2, (0,))):
        def send_others(p):
            @pl.when(p != group)
            def _():
                send(h, p, which)

        in_order(LAST_SENDS if h == LOCAL_HEADS - 1 else SENDS, send_others)
        if 0 in which:
            own(h)

    for table in tables:
        table.wait()

    @pl.when(rank > 0)
    def _():
        pl.semaphore_wait(sibling_ready, rank)

    def attend(h, slot):
        block = slot * ranks + rank
        g0, g1 = glob_ref[0], glob_ref[1]

        def bias(b, inside):
            ok = inside & (b != g0) & (b != g1)
            return jnp.where(ok, jnp.float32(0.0), jnp.float32(NEG))

        ids = [
            jnp.maximum(block - 1, 0),
            block,
            jnp.minimum(block + 1, blocks - 1),
            g0,
            g1,
        ] + [rand_ref[r, block] for r in range(RANDOMS)]
        biases = [
            bias(block - 1, block >= 1),
            bias(block, block >= 0),
            bias(block + 1, block + 1 < blocks),
        ]
        query = qs[h, slot]
        slots = [lax.rem(i, ranks) * GROUPS + lax.div(i, ranks) for i in ids]
        key = jnp.concatenate([kvs[h][i, 0] for i in slots], axis=0)
        value = jnp.concatenate([kvs[h][i, 1] for i in slots], axis=0)
        scores = lax.dot_general(
            query, key, (((1,), (1,)), ((), ())), preferred_element_type=jnp.float32
        ) * (HEAD_DIM ** -0.5)
        parts = [scores[:, n * BLOCK : (n + 1) * BLOCK] for n in range(len(ids))]
        parts = [part + biases[n] if n < 3 else part for n, part in enumerate(parts)]
        top = jnp.max(functools.reduce(jnp.maximum, parts), axis=1, keepdims=True)
        powers = [jnp.exp(part - top) for part in parts]
        total = jnp.sum(functools.reduce(jnp.add, powers), axis=1, keepdims=True)
        inverse = 1.0 / total
        probs = jnp.concatenate([(power * inverse).astype(jnp.bfloat16) for power in powers], axis=1)
        result = lax.dot_general(
            probs, value, (((1,), (0,)), ((), ())), preferred_element_type=jnp.float32
        )
        os[h, slot] = result.astype(jnp.bfloat16)

    upper = group >= GROUPS // 2
    inner = (group >= GROUPS // 4) & (group < GROUPS - GROUPS // 4)
    last = LOCAL_HEADS - 1

    def beside(q):
        return jnp.where(group == GROUPS // 2, GROUPS // 2 + 1 - q, q) if q >= GROUPS // 4 else q

    for h in range(LOCAL_HEADS):
        wait_bytes(mine(h), kv_recv.at[h])

        @pl.loop(1, ranks)
        def _(i):
            if h > 0:
                wait_bytes(mine(h), fwd_send.at[i - 1])
            forward(h, i)

        wait_bytes(qs.at[h], q_recv.at[h])
        wait_bytes(kvs[h].at[pl.ds(0, (ranks - 1) * GROUPS)], fwd_recv.at[h])

        if h == last:
            @pl.when(jnp.logical_not(inner))
            def _():
                for earlier in range(last):
                    @pl.loop(0, GROUPS // 2)
                    def _(k):
                        send_out(earlier, k + jnp.where(upper, 0, GROUPS // 2))

        def attend_and_send(p):
            attend(h, p)
            now = p != group
            if h < last:
                now &= inner | ((p >= GROUPS // 2) == upper)
            held = [q for q, heads in HELD.items() if h in heads]
            if held:
                now &= jnp.logical_not(inner & upper & functools.reduce(jnp.logical_or, [p == beside(q) for q in held]))

            @pl.when(now)
            def _():
                send_out(h, p)

            if h == last:
                for trigger, results in RELEASED.items():
                    @pl.when(inner & upper & (p == beside(trigger)))
                    def _():
                        for earlier, q in results:
                            send_out(earlier, beside(q))

        in_order(RESULTS, attend_and_send)
        out_local(h)

    sent = os.at[:, pl.ds(0, GROUPS - 1)]
    for t in (1, 2, 0):
        wait_bytes(sent, send_sem.at[t])

    @pl.loop(1, ranks)
    def _(i):
        wait_bytes(mine(last), fwd_send.at[i - 1])

    wait_bytes(sent, out_send)
    wait_bytes(out_hbm, out_recv)


def local(queries, keys, values, rand_blocks, global_ids):
    seq = lax.axis_size("seq")
    ranks = seq // GROUPS
    blocks = rand_blocks.shape[0]
    assert queries.shape[0] == BLOCK and blocks == seq and seq % GROUPS == 0
    tile = (BLOCK, HEAD_DIM)
    sources = [pltpu.with_memory_space_constraint(x, pltpu.MemorySpace.HBM) for x in (rand_blocks.T, global_ids, queries, keys, values)]
    anywhere = pl.BlockSpec(memory_space=pl.ANY)
    dma = pltpu.SemaphoreType.DMA
    return pl.pallas_call(
        functools.partial(kernel, ranks),
        out_shape=jax.ShapeDtypeStruct(queries.shape, jnp.bfloat16),
        in_specs=[anywhere] * 5,
        out_specs=anywhere,
        scratch_shapes=[
            pltpu.VMEM((LOCAL_HEADS, GROUPS) + tile, jnp.bfloat16),
            pltpu.VMEM((LOCAL_HEADS, GROUPS) + tile, jnp.bfloat16),
            pltpu.SMEM((RANDOMS, blocks), jnp.int32),
            pltpu.SMEM((GLOBALS,), jnp.int32),
        ]
        + [pltpu.VMEM((blocks, 2) + tile, jnp.bfloat16)] * LOCAL_HEADS
        + [
            dma((3,)),
            dma((LOCAL_HEADS,)),
            dma((LOCAL_HEADS,)),
            dma((ranks - 1,)),
            dma((LOCAL_HEADS,)),
            dma,
            dma,
            pltpu.SemaphoreType.REGULAR((GROUPS - 1,)),
            pltpu.SemaphoreType.REGULAR,
        ],
        compiler_params=pltpu.CompilerParams(
            collective_id=0, has_side_effects=True, vmem_limit_bytes=40 << 20
        ),
    )(*sources)


def solution(mesh):
    placed = (
        P(("groups", "seq"), None),
        P(("groups", "seq"), None),
        P(("groups", "seq"), None),
        P("groups", None),
        P("groups"),
    )
    return jax.shard_map(
        local, mesh=mesh, in_specs=placed, out_specs=P(("groups", "seq"), None), check_vma=False
    )
```

```python
import functools

import jax
import jax.numpy as jnp
from jax import lax
from jax.experimental import pallas as pl
from jax.experimental.pallas import tpu as pltpu
from jax.sharding import PartitionSpec as P

HEADS = 24
HEAD_DIM = 128
BLOCK = 128
GLOBALS = 2
RANDOMS = 3
LOCAL_HEADS = 3
GROUPS = HEADS // LOCAL_HEADS
MESH = pl.DeviceIdType.MESH
NEG = -1e30


SENDS = (
    (5, 4, 7, 6, 2, 3, 1, 0),
    (5, 4, 7, 6, 3, 2, 0, 1),
    (5, 4, 7, 6, 0, 1, 3, 2),
    (5, 4, 7, 6, 0, 1, 2, 3),
    (3, 2, 1, 0, 6, 7, 5, 4),
    (3, 2, 1, 0, 6, 7, 4, 5),
    (3, 2, 1, 0, 4, 5, 7, 6),
    (3, 2, 1, 0, 4, 5, 6, 7),
)
RESULTS = (
    (4, 6, 5, 7, 2, 1, 3, 0),
    (4, 6, 5, 7, 0, 2, 3, 1),
    (0, 1, 4, 6, 7, 5, 3, 2),
    (0, 2, 1, 4, 6, 7, 5, 3),
    (0, 1, 3, 2, 6, 7, 5, 4),
    (0, 1, 2, 3, 4, 6, 7, 5),
    (0, 1, 2, 3, 4, 5, 7, 6),
    (0, 1, 2, 3, 4, 5, 6, 7),
)
HELD = {1: (1,), 2: (1,), 3: (0, 1)}
RELEASED = {0: ((1, 1), (1, 2)), 2: ((0, 3), (1, 3))}
SIGNALS = (
    (5, 4, 3, 2, 1, 7, 6),
    (0, 2, 3, 5, 6, 7),
    (4, 5, 3, 6, 7),
    (5, 6, 7),
    (2, 3, 1, 6, 7),
    (3, 6, 7),
    (7,),
    (6,),
)
HEARD = ((1,), (4, 0), (4, 0, 1), (5, 4, 2, 0, 1), (2, 0), (3, 2, 1, 0), (0, 1, 2, 3, 4, 5, 7), (0, 1, 2, 3, 4, 5, 6))
LATER = ((4, 2, 5, 3, 7, 6), (2, 5, 3, 7, 6), (5, 3, 7, 6), (7, 6), (3, 5, 1, 7, 6), (4, 7, 6), (), ())
TELLS = ((), (4,), (0, 1), (5, 0, 1, 2, 4), (0,), (0, 1, 2), (0, 1, 2, 3, 4, 5), (0, 1, 2, 3, 4, 5))


def kernel(ranks, rand_hbm, glob_hbm, q_hbm, k_hbm, v_hbm, out_hbm, qs, os, rand_ref, glob_ref, *scratch):
    kvs = scratch[:LOCAL_HEADS]
    (send_sem, q_recv, kv_recv, fwd_send, fwd_recv, out_send, out_recv, ready, sibling_ready) = scratch[LOCAL_HEADS:]
    rollout = lax.axis_index("groups")
    me = lax.axis_index("seq")
    group, rank = lax.div(me, ranks), lax.rem(me, ranks)
    blocks = ranks * GROUPS
    def sibling(i):
        return group * ranks + lax.rem(rank + i, ranks)

    def device(index):
        return (rollout, index)

    def pick(values):
        return functools.reduce(lambda rest, g: jnp.where(group == g, values[g], rest), range(1, GROUPS), values[0])

    def in_order(rows, body):
        code = pick([sum(p << 3 * k for k, p in enumerate(row)) for row in rows])

        @pl.loop(0, pick([len(row) for row in rows]))
        def _(k):
            body(lax.shift_right_logical(code, 3 * k) & 7)

    barrier = pltpu.get_barrier_semaphore()

    def signal(semaphore, index):
        pl.semaphore_signal(semaphore, inc=1, device_id=device(index), device_id_type=MESH)

    in_order(SIGNALS, lambda p: signal(barrier, p * ranks + rank))

    @pl.loop(0, rank)
    def _(i):
        signal(barrier, group * ranks + i)

    tables = (
        pltpu.make_async_copy(rand_hbm, rand_ref, fwd_send.at[0]),
        pltpu.make_async_copy(glob_hbm, glob_ref, out_send),
    )
    for table in tables:
        table.start()

    sources = (q_hbm, k_hbm, v_hbm)

    def columns(owner, h):
        start = pl.multiple_of((owner * LOCAL_HEADS + h) * HEAD_DIM, HEAD_DIM)
        return pl.ds(start, HEAD_DIM)

    def slab(t, h, owner_group):
        if t == 0:
            return qs.at[h, owner_group]
        return kvs[h].at[rank * GROUPS + owner_group, t - 1]

    def send(h, p, which=(1, 2, 0)):
        for t in which:
            pltpu.make_async_remote_copy(
                src_ref=sources[t].at[:, columns(p, h)],
                dst_ref=slab(t, h, group),
                send_sem=send_sem.at[t],
                recv_sem=(q_recv if t == 0 else kv_recv).at[h],
                device_id=device(p * ranks + rank),
                device_id_type=MESH,
            ).start()

    def own(h):
        for t in (1, 2, 0):
            pltpu.make_async_copy(
                sources[t].at[:, columns(group, h)], slab(t, h, group), (q_recv if t == 0 else kv_recv).at[h]
            ).start()

    def mine(h):
        return kvs[h].at[pl.ds(rank * GROUPS, GROUPS)]

    def forward(h, i):
        pltpu.make_async_remote_copy(
            src_ref=mine(h),
            dst_ref=mine(h),
            send_sem=fwd_send.at[i - 1],
            recv_sem=fwd_recv.at[h],
            device_id=device(sibling(i)),
            device_id_type=MESH,
        ).start()

    def send_out(h, p):
        pltpu.make_async_remote_copy(
            src_ref=os.at[h, p],
            dst_ref=out_hbm.at[:, columns(group, h)],
            send_sem=out_send,
            recv_sem=out_recv,
            device_id=device(p * ranks + rank),
            device_id_type=MESH,
        ).start()

    def out_local(h):
        pltpu.make_async_copy(os.at[h, group], out_hbm.at[:, columns(group, h)], out_recv).start()

    def wait_bytes(ref, sem):
        pltpu.make_async_copy(ref, ref, sem).wait()

    pl.semaphore_wait(barrier, pick([len(row) for row in HEARD]) + ranks - 1 - rank)

    in_order(TELLS, lambda p: signal(ready.at[jnp.minimum(group, GROUPS - 2)], p * ranks + rank))
    in_order(HEARD, lambda p: send(0, p))

    @pl.loop(rank + 1, ranks)
    def _(i):
        signal(sibling_ready, group * ranks + i)

    own(0)

    def send_later(p):
        @pl.when((p < GROUPS - 2) & jnp.logical_not((group == 4) & (p == 5)))
        def _():
            pl.semaphore_wait(ready.at[jnp.where((group == 5) & (p == 4), 3, p)], 1)

        @pl.when(p == GROUPS - 1)
        def _():
            pl.semaphore_wait(ready.at[GROUPS - 2], 2)

        send(0, p)

    in_order(LATER, send_later)

    for h, which in ((1, (1, 2, 0)), (2, (1, 2)), (2, (0,))):
        def send_others(p):
            @pl.when(p != group)
            def _():
                send(h, p, which)

        in_order(SENDS, send_others)
        if 0 in which:
            own(h)

    for table in tables:
        table.wait()

    @pl.when(rank > 0)
    def _():
        pl.semaphore_wait(sibling_ready, rank)

    def attend(h, slot):
        block = slot * ranks + rank
        g0, g1 = glob_ref[0], glob_ref[1]

        def bias(b, inside):
            ok = inside & (b != g0) & (b != g1)
            return jnp.where(ok, jnp.float32(0.0), jnp.float32(NEG))

        ids = [
            jnp.maximum(block - 1, 0),
            block,
            jnp.minimum(block + 1, blocks - 1),
            g0,
            g1,
        ] + [rand_ref[r, block] for r in range(RANDOMS)]
        biases = [
            bias(block - 1, block >= 1),
            bias(block, block >= 0),
            bias(block + 1, block + 1 < blocks),
        ]
        query = qs[h, slot]
        slots = [lax.rem(i, ranks) * GROUPS + lax.div(i, ranks) for i in ids]
        key = jnp.concatenate([kvs[h][i, 0] for i in slots], axis=0)
        value = jnp.concatenate([kvs[h][i, 1] for i in slots], axis=0)
        scores = lax.dot_general(
            query, key, (((1,), (1,)), ((), ())), preferred_element_type=jnp.float32
        ) * (HEAD_DIM ** -0.5)
        parts = [scores[:, n * BLOCK : (n + 1) * BLOCK] for n in range(len(ids))]
        parts = [part + biases[n] if n < 3 else part for n, part in enumerate(parts)]
        top = jnp.max(functools.reduce(jnp.maximum, parts), axis=1, keepdims=True)
        powers = [jnp.exp(part - top) for part in parts]
        total = jnp.sum(functools.reduce(jnp.add, powers), axis=1, keepdims=True)
        inverse = 1.0 / total
        probs = jnp.concatenate([(power * inverse).astype(jnp.bfloat16) for power in powers], axis=1)
        result = lax.dot_general(
            probs, value, (((1,), (0,)), ((), ())), preferred_element_type=jnp.float32
        )
        os[h, slot] = result.astype(jnp.bfloat16)

    upper = group >= GROUPS // 2
    inner = (group >= GROUPS // 4) & (group < GROUPS - GROUPS // 4)
    last = LOCAL_HEADS - 1

    def beside(q):
        return jnp.where(group == GROUPS // 2, GROUPS // 2 + 1 - q, q) if q >= GROUPS // 4 else q

    for h in range(LOCAL_HEADS):
        wait_bytes(mine(h), kv_recv.at[h])

        @pl.loop(1, ranks)
        def _(i):
            if h > 0:
                wait_bytes(mine(h), fwd_send.at[i - 1])
            forward(h, i)

        wait_bytes(qs.at[h], q_recv.at[h])
        wait_bytes(kvs[h].at[pl.ds(0, (ranks - 1) * GROUPS)], fwd_recv.at[h])

        if h == last:
            @pl.when(jnp.logical_not(inner))
            def _():
                for earlier in range(last):
                    @pl.loop(0, GROUPS // 2)
                    def _(k):
                        send_out(earlier, k + jnp.where(upper, 0, GROUPS // 2))

        def attend_and_send(p):
            attend(h, p)
            now = p != group
            if h < last:
                now &= inner | ((p >= GROUPS // 2) == upper)
            held = [q for q, heads in HELD.items() if h in heads]
            if held:
                now &= jnp.logical_not(inner & upper & functools.reduce(jnp.logical_or, [p == beside(q) for q in held]))

            @pl.when(now)
            def _():
                send_out(h, p)

            if h == last:
                for trigger, results in RELEASED.items():
                    @pl.when(inner & upper & (p == beside(trigger)))
                    def _():
                        for earlier, q in results:
                            send_out(earlier, beside(q))

        in_order(RESULTS, attend_and_send)
        out_local(h)

    sent = os.at[:, pl.ds(0, GROUPS - 1)]
    for t in (1, 2, 0):
        wait_bytes(sent, send_sem.at[t])

    @pl.loop(1, ranks)
    def _(i):
        wait_bytes(mine(last), fwd_send.at[i - 1])

    wait_bytes(sent, out_send)
    wait_bytes(out_hbm, out_recv)


def local(queries, keys, values, rand_blocks, global_ids):
    seq = lax.axis_size("seq")
    ranks = seq // GROUPS
    blocks = rand_blocks.shape[0]
    assert queries.shape[0] == BLOCK and blocks == seq and seq % GROUPS == 0
    tile = (BLOCK, HEAD_DIM)
    sources = [pltpu.with_memory_space_constraint(x, pltpu.MemorySpace.HBM) for x in (rand_blocks.T, global_ids, queries, keys, values)]
    anywhere = pl.BlockSpec(memory_space=pl.ANY)
    dma = pltpu.SemaphoreType.DMA
    return pl.pallas_call(
        functools.partial(kernel, ranks),
        out_shape=jax.ShapeDtypeStruct(queries.shape, jnp.bfloat16),
        in_specs=[anywhere] * 5,
        out_specs=anywhere,
        scratch_shapes=[
            pltpu.VMEM((LOCAL_HEADS, GROUPS) + tile, jnp.bfloat16),
            pltpu.VMEM((LOCAL_HEADS, GROUPS) + tile, jnp.bfloat16),
            pltpu.SMEM((RANDOMS, blocks), jnp.int32),
            pltpu.SMEM((GLOBALS,), jnp.int32),
        ]
        + [pltpu.VMEM((blocks, 2) + tile, jnp.bfloat16)] * LOCAL_HEADS
        + [
            dma((3,)),
            dma((LOCAL_HEADS,)),
            dma((LOCAL_HEADS,)),
            dma((ranks - 1,)),
            dma((LOCAL_HEADS,)),
            dma,
            dma,
            pltpu.SemaphoreType.REGULAR((GROUPS - 1,)),
            pltpu.SemaphoreType.REGULAR,
        ],
        compiler_params=pltpu.CompilerParams(
            collective_id=0, has_side_effects=True, vmem_limit_bytes=40 << 20
        ),
    )(*sources)


def solution(mesh):
    placed = (
        P(("groups", "seq"), None),
        P(("groups", "seq"), None),
        P(("groups", "seq"), None),
        P("groups", None),
        P("groups"),
    )
    return jax.shard_map(
        local, mesh=mesh, in_specs=placed, out_specs=P(("groups", "seq"), None), check_vma=False
    )
```

```python
import functools

import jax
import jax.numpy as jnp
from jax import lax
from jax.experimental import pallas as pl
from jax.experimental.pallas import tpu as pltpu
from jax.sharding import PartitionSpec as P

HEADS = 24
HEAD_DIM = 128
BLOCK = 128
GLOBALS = 2
RANDOMS = 3
LOCAL_HEADS = 3
GROUPS = HEADS // LOCAL_HEADS
MESH = pl.DeviceIdType.MESH
NEG = -1e30


SENDS = (
    (6, 7, 4, 5, 2, 3, 1, 0),
    (7, 6, 4, 5, 3, 2, 0, 1),
    (6, 7, 4, 5, 0, 1, 3, 2),
    (6, 7, 4, 5, 0, 1, 2, 3),
    (0, 1, 2, 3, 6, 7, 5, 4),
    (0, 1, 2, 3, 6, 7, 4, 5),
    (0, 1, 2, 3, 4, 5, 7, 6),
    (0, 1, 2, 3, 4, 5, 6, 7),
)
LAST_SENDS = (
    (5, 4, 7, 6, 2, 3, 1, 0),
    (5, 4, 7, 6, 3, 2, 0, 1),
    (5, 4, 7, 6, 0, 1, 3, 2),
    (5, 4, 7, 6, 0, 1, 2, 3),
    (3, 2, 1, 0, 6, 7, 5, 4),
    (3, 2, 1, 0, 6, 7, 4, 5),
    (3, 2, 1, 0, 4, 5, 7, 6),
    (3, 2, 1, 0, 4, 5, 6, 7),
)
RESULTS = (
    (4, 6, 5, 7, 2, 1, 3, 0),
    (4, 6, 5, 7, 0, 2, 3, 1),
    (0, 1, 4, 6, 7, 5, 3, 2),
    (0, 2, 1, 4, 6, 5, 7, 3),
    (0, 1, 3, 2, 6, 7, 5, 4),
    (0, 1, 2, 3, 4, 6, 7, 5),
    (0, 1, 2, 3, 4, 5, 7, 6),
    (0, 1, 2, 3, 4, 5, 6, 7),
)
HELD = {1: (1,), 2: (1,), 3: (0, 1)}
RELEASED = {0: ((1, 1), (1, 2)), 2: ((0, 3), (1, 3))}
SIGNALS = (
    (5, 4, 3, 2, 1, 7, 6),
    (0, 2, 3, 5, 6, 7),
    (4, 5, 3, 6, 7),
    (5, 6, 7),
    (2, 3, 1, 6, 7),
    (3, 6, 7),
    (7,),
    (6,),
)
HEARD = ((1,), (4, 0), (4, 0, 1), (5, 4, 2, 0, 1), (2, 0), (3, 2, 1, 0), (0, 1, 2, 3, 4, 5, 7), (0, 1, 2, 3, 4, 5, 6))
LATER = ((4, 2, 5, 3, 7, 6), (2, 5, 3, 7, 6), (5, 3, 7, 6), (7, 6), (3, 5, 1, 7, 6), (4, 7, 6), (), ())
TELLS = ((), (4,), (0, 1), (5, 0, 1, 2, 4), (0,), (0, 1, 2), (0, 1, 2, 3, 4, 5), (0, 1, 2, 3, 4, 5))


def kernel(ranks, rand_hbm, glob_hbm, q_hbm, k_hbm, v_hbm, out_hbm, qs, os, rand_ref, glob_ref, *scratch):
    kvs = scratch[:LOCAL_HEADS]
    (send_sem, q_recv, kv_recv, fwd_send, fwd_recv, out_send, out_recv, ready, sibling_ready) = scratch[LOCAL_HEADS:]
    rollout = lax.axis_index("groups")
    me = lax.axis_index("seq")
    group, rank = lax.div(me, ranks), lax.rem(me, ranks)
    blocks = ranks * GROUPS
    def sibling(i):
        return group * ranks + lax.rem(rank + i, ranks)

    def device(index):
        return (rollout, index)

    def pick(values):
        return functools.reduce(lambda rest, g: jnp.where(group == g, values[g], rest), range(1, GROUPS), values[0])

    def in_order(rows, body):
        code = pick([sum(p << 3 * k for k, p in enumerate(row)) for row in rows])

        @pl.loop(0, pick([len(row) for row in rows]))
        def _(k):
            body(lax.shift_right_logical(code, 3 * k) & 7)

    barrier = pltpu.get_barrier_semaphore()

    def signal(semaphore, index):
        pl.semaphore_signal(semaphore, inc=1, device_id=device(index), device_id_type=MESH)

    in_order(SIGNALS, lambda p: signal(barrier, p * ranks + rank))

    @pl.loop(0, rank)
    def _(i):
        signal(barrier, group * ranks + i)

    tables = (
        pltpu.make_async_copy(rand_hbm, rand_ref, fwd_send.at[0]),
        pltpu.make_async_copy(glob_hbm, glob_ref, out_send),
    )
    for table in tables:
        table.start()

    sources = (q_hbm, k_hbm, v_hbm)

    def columns(owner, h):
        start = pl.multiple_of((owner * LOCAL_HEADS + h) * HEAD_DIM, HEAD_DIM)
        return pl.ds(start, HEAD_DIM)

    def slab(t, h, owner_group):
        if t == 0:
            return qs.at[h, owner_group]
        return kvs[h].at[rank * GROUPS + owner_group, t - 1]

    def send(h, p, which=(1, 2, 0)):
        for t in which:
            pltpu.make_async_remote_copy(
                src_ref=sources[t].at[:, columns(p, h)],
                dst_ref=slab(t, h, group),
                send_sem=send_sem.at[t],
                recv_sem=(q_recv if t == 0 else kv_recv).at[h],
                device_id=device(p * ranks + rank),
                device_id_type=MESH,
            ).start()

    def own(h):
        for t in (1, 2, 0):
            pltpu.make_async_copy(
                sources[t].at[:, columns(group, h)], slab(t, h, group), (q_recv if t == 0 else kv_recv).at[h]
            ).start()

    def mine(h):
        return kvs[h].at[pl.ds(rank * GROUPS, GROUPS)]

    def forward(h, i):
        pltpu.make_async_remote_copy(
            src_ref=mine(h),
            dst_ref=mine(h),
            send_sem=fwd_send.at[i - 1],
            recv_sem=fwd_recv.at[h],
            device_id=device(sibling(i)),
            device_id_type=MESH,
        ).start()

    def send_out(h, p):
        pltpu.make_async_remote_copy(
            src_ref=os.at[h, p],
            dst_ref=out_hbm.at[:, columns(group, h)],
            send_sem=out_send,
            recv_sem=out_recv,
            device_id=device(p * ranks + rank),
            device_id_type=MESH,
        ).start()

    def out_local(h):
        pltpu.make_async_copy(os.at[h, group], out_hbm.at[:, columns(group, h)], out_recv).start()

    def wait_bytes(ref, sem):
        pltpu.make_async_copy(ref, ref, sem).wait()

    pl.semaphore_wait(barrier, pick([len(row) for row in HEARD]) + ranks - 1 - rank)

    in_order(TELLS, lambda p: signal(ready.at[jnp.minimum(group, GROUPS - 2)], p * ranks + rank))
    in_order(HEARD, lambda p: send(0, p))

    @pl.loop(rank + 1, ranks)
    def _(i):
        signal(sibling_ready, group * ranks + i)

    own(0)

    def send_later(p):
        @pl.when((p < GROUPS - 2) & jnp.logical_not((group == 4) & (p == 5)))
        def _():
            pl.semaphore_wait(ready.at[jnp.where((group == 5) & (p == 4), 3, p)], 1)

        @pl.when(p == GROUPS - 1)
        def _():
            pl.semaphore_wait(ready.at[GROUPS - 2], 2)

        send(0, p)

    in_order(LATER, send_later)

    for h, which in ((1, (1, 2)), (1, (0,)), (2, (1, 2)), (2, (0,))):
        def send_others(p):
            @pl.when(p != group)
            def _():
                send(h, p, which)

        in_order(LAST_SENDS if h == LOCAL_HEADS - 1 else SENDS, send_others)
        if 0 in which:
            own(h)

    for table in tables:
        table.wait()

    @pl.when(rank > 0)
    def _():
        pl.semaphore_wait(sibling_ready, rank)

    def attend(h, slot):
        block = slot * ranks + rank
        g0, g1 = glob_ref[0], glob_ref[1]

        def bias(b, inside):
            ok = inside & (b != g0) & (b != g1)
            return jnp.where(ok, jnp.float32(0.0), jnp.float32(NEG))

        ids = [
            jnp.maximum(block - 1, 0),
            block,
            jnp.minimum(block + 1, blocks - 1),
            g0,
            g1,
        ] + [rand_ref[r, block] for r in range(RANDOMS)]
        biases = [
            bias(block - 1, block >= 1),
            bias(block, block >= 0),
            bias(block + 1, block + 1 < blocks),
        ]
        query = qs[h, slot]
        slots = [lax.rem(i, ranks) * GROUPS + lax.div(i, ranks) for i in ids]
        key = jnp.concatenate([kvs[h][i, 0] for i in slots], axis=0)
        value = jnp.concatenate([kvs[h][i, 1] for i in slots], axis=0)
        scores = lax.dot_general(
            query, key, (((1,), (1,)), ((), ())), preferred_element_type=jnp.float32
        ) * (HEAD_DIM ** -0.5)
        parts = [scores[:, n * BLOCK : (n + 1) * BLOCK] for n in range(len(ids))]
        parts = [part + biases[n] if n < 3 else part for n, part in enumerate(parts)]
        top = jnp.max(functools.reduce(jnp.maximum, parts), axis=1, keepdims=True)
        powers = [jnp.exp(part - top) for part in parts]
        total = jnp.sum(functools.reduce(jnp.add, powers), axis=1, keepdims=True)
        inverse = 1.0 / total
        probs = jnp.concatenate([(power * inverse).astype(jnp.bfloat16) for power in powers], axis=1)
        result = lax.dot_general(
            probs, value, (((1,), (0,)), ((), ())), preferred_element_type=jnp.float32
        )
        os[h, slot] = result.astype(jnp.bfloat16)

    upper = group >= GROUPS // 2
    inner = (group >= GROUPS // 4) & (group < GROUPS - GROUPS // 4)
    last = LOCAL_HEADS - 1

    def beside(q):
        return jnp.where(group == GROUPS // 2, GROUPS // 2 + 1 - q, q) if q >= GROUPS // 4 else q

    for h in range(LOCAL_HEADS):
        wait_bytes(mine(h), kv_recv.at[h])

        @pl.loop(1, ranks)
        def _(i):
            if h > 0:
                wait_bytes(mine(h), fwd_send.at[i - 1])
            forward(h, i)

        wait_bytes(qs.at[h], q_recv.at[h])
        wait_bytes(kvs[h].at[pl.ds(0, (ranks - 1) * GROUPS)], fwd_recv.at[h])

        if h == last:
            @pl.when(jnp.logical_not(inner))
            def _():
                for earlier in range(last):
                    @pl.loop(0, GROUPS // 2)
                    def _(k):
                        send_out(earlier, k + jnp.where(upper, 0, GROUPS // 2))

        def attend_and_send(p):
            attend(h, p)
            now = p != group
            if h < last:
                now &= inner | ((p >= GROUPS // 2) == upper)
            held = [q for q, heads in HELD.items() if h in heads]
            if held:
                now &= jnp.logical_not(inner & upper & functools.reduce(jnp.logical_or, [p == beside(q) for q in held]))

            @pl.when(now)
            def _():
                send_out(h, p)

            if h == last:
                for trigger, results in RELEASED.items():
                    @pl.when(inner & upper & (p == beside(trigger)))
                    def _():
                        for earlier, q in results:
                            send_out(earlier, beside(q))

        in_order(RESULTS, attend_and_send)
        out_local(h)

    sent = os.at[:, pl.ds(0, GROUPS - 1)]
    for t in (1, 2, 0):
        wait_bytes(sent, send_sem.at[t])

    @pl.loop(1, ranks)
    def _(i):
        wait_bytes(mine(last), fwd_send.at[i - 1])

    wait_bytes(sent, out_send)
    wait_bytes(out_hbm, out_recv)


def local(queries, keys, values, rand_blocks, global_ids):
    seq = lax.axis_size("seq")
    ranks = seq // GROUPS
    blocks = rand_blocks.shape[0]
    assert queries.shape[0] == BLOCK and blocks == seq and seq % GROUPS == 0
    tile = (BLOCK, HEAD_DIM)
    sources = [pltpu.with_memory_space_constraint(x, pltpu.MemorySpace.HBM) for x in (rand_blocks.T, global_ids, queries, keys, values)]
    anywhere = pl.BlockSpec(memory_space=pl.ANY)
    dma = pltpu.SemaphoreType.DMA
    return pl.pallas_call(
        functools.partial(kernel, ranks),
        out_shape=jax.ShapeDtypeStruct(queries.shape, jnp.bfloat16),
        in_specs=[anywhere] * 5,
        out_specs=anywhere,
        scratch_shapes=[
            pltpu.VMEM((LOCAL_HEADS, GROUPS) + tile, jnp.bfloat16),
            pltpu.VMEM((LOCAL_HEADS, GROUPS) + tile, jnp.bfloat16),
            pltpu.SMEM((RANDOMS, blocks), jnp.int32),
            pltpu.SMEM((GLOBALS,), jnp.int32),
        ]
        + [pltpu.VMEM((blocks, 2) + tile, jnp.bfloat16)] * LOCAL_HEADS
        + [
            dma((3,)),
            dma((LOCAL_HEADS,)),
            dma((LOCAL_HEADS,)),
            dma((ranks - 1,)),
            dma((LOCAL_HEADS,)),
            dma,
            dma,
            pltpu.SemaphoreType.REGULAR((GROUPS - 1,)),
            pltpu.SemaphoreType.REGULAR,
        ],
        compiler_params=pltpu.CompilerParams(
            collective_id=0, has_side_effects=True, vmem_limit_bytes=40 << 20
        ),
    )(*sources)


def solution(mesh):
    placed = (
        P(("groups", "seq"), None),
        P(("groups", "seq"), None),
        P(("groups", "seq"), None),
        P("groups", None),
        P("groups"),
    )
    return jax.shard_map(
        local, mesh=mesh, in_specs=placed, out_specs=P(("groups", "seq"), None), check_vma=False
    )
```
